256 devices in a mesh: rows: 32 (over x, z_lo, core), cols: 8 (over y, z_hi).
Axes of the slice: x: 4, y: 4, z: 8 (z_hi: 2, z_lo: 4; z = z_hi * 4 + z_lo), core: 2. Of those that a mesh axis runs over, the one named last changes fastest.
Arguments:
- matrix_blocks: bfloat16 [8192, 64, 1728], P(('rows', 'cols')), may hold values from -0.75 to 0.75
- restrict: bfloat16 [8192, 4096], P(('rows', 'cols')), may hold values from -1.5 to 1.5
- columns: int32 [8192, 27], P(('rows', 'cols')), may hold values from 0 to 767
- counts: int32 [8192], P(('rows', 'cols')), may hold values from 8 to 27, as said below
- aggregate: int32 [8192], P(('rows', 'cols')), may hold values from 0 to 1
Outputs:
- coarse: float32 [512, 64, 3072], P(('rows', 'cols'))
The draws below stay inside these ranges and needn't reach their ends.
Inputs may be any that keep to these rules, and one draw needn't show every extreme that they name: `counts`: used slots are the first ones of a row; some row uses all 27.
All inputs are finite; a program needn't handle non-finite values.
Results may differ from the reference program's by a relative error of at most 0.0029.
Values may be sent and summed in bfloat16 or wider, within the bound.
A program may use at most 192 MiB of HBM per device.

```python
import jax
import jax.numpy as jnp
from jax import lax

BLK = 64
SLOTS = 27
ROWS_DEV = 32
AGG_DEV = 2
SLAB = 256
WINDOW = 48
FINE = 8192
COARSE = 512
N_COLS = 8


def draw_counts(key, part):
    cap_key, row_key = jax.random.split(jax.random.fold_in(key, 11))
    blocks = FINE // ROWS_DEV
    caps = jax.random.randint(cap_key, (blocks,), 14, SLOTS + 1)
    caps = caps.at[0].set(SLOTS)
    per_row = jnp.repeat(caps, ROWS_DEV)
    raw_bits = jax.random.randint(row_key, (FINE,), 0, 1 << 20)
    row_counts = 8 + raw_bits % (per_row - 7)
    row_counts = row_counts.at[0].set(SLOTS)
    return row_counts.astype(jnp.int32)


def set_ends(drawn, stream_key, smallest, high):
    extent = drawn.shape
    spot = [jax.random.randint(jax.random.fold_in(stream_key, axis), (), 0, extent[axis]) for axis in range(len(extent))]
    drawn = drawn.at[tuple(spot)].set(smallest)
    longest = extent.index(max(extent))
    spot[longest] = (spot[longest] + 1) % extent[longest]
    return drawn.at[tuple(spot)].set(high)


def level_of(stream_key, dims, cuts, smallest, largest):
    def one(position, shards_of):
        draws = jax.random.uniform(jax.random.fold_in(jax.random.fold_in(stream_key, 6), position), (shards_of,), jnp.float32, smallest / len(cuts), largest / len(cuts))
        return jnp.repeat(jnp.exp(draws), dims[position] // shards_of).reshape((-1,) + (1,) * (len(dims) - position - 1))

    gain = one(*cuts[0])
    for cut in cuts[1:]:
        gain = gain * one(*cut)
    return gain


def normal_values(key, extent, width, limit, cuts=(), kind=jnp.bfloat16):
    array = jax.random.normal(key, extent, jnp.float32) * width
    if len(cuts) > 0:
        array = level_of(key, extent, cuts, -0.22, 0.18) * array
    return jnp.clip(array, min=-limit, max=limit).astype(kind)


def setup_inputs(seed: int = 0) -> dict:
    key_list = jax.random.split(jax.random.key(seed), 6)
    return {
        "matrix_blocks": normal_values(key_list[0], (FINE, BLK, SLOTS * BLK), BLK ** -0.5, 0.75, ((0, 256),)),
        "restrict": normal_values(key_list[1], (FINE, BLK * BLK), 0.25, 1.5, ((0, 256),)),
        "columns": set_ends(jax.random.randint(key_list[2], (FINE, SLOTS), 0, 3 * SLAB), jax.random.fold_in(key_list[2], 1), 0, (3 * SLAB) - 1).astype(jnp.int32),
        "counts": draw_counts(jax.random.fold_in(key_list[5], 71), 0),
        "aggregate": set_ends(jax.random.randint(key_list[4], (FINE,), 0, AGG_DEV), jax.random.fold_in(key_list[4], 1), 0, AGG_DEV - 1).astype(jnp.int32),
    }


def reference(matrix_blocks, restrict, columns, counts, aggregate):
    blocks = FINE // ROWS_DEV

    def one_device(device):
        first_row = device * ROWS_DEV
        a_rows = lax.dynamic_slice_in_dim(matrix_blocks, first_row, ROWS_DEV, 0)
        r_rows = lax.dynamic_slice_in_dim(restrict, first_row, ROWS_DEV, 0).reshape(ROWS_DEV, BLK, BLK)
        row_cols = lax.dynamic_slice_in_dim(columns, first_row, ROWS_DEV, 0)
        row_counts = lax.dynamic_slice_in_dim(counts, first_row, ROWS_DEV, 0)
        row_agg = lax.dynamic_slice_in_dim(aggregate, first_row, ROWS_DEV, 0)
        slab_index = device // N_COLS
        global_row = (slab_index - 1) * SLAB + row_cols
        slot_index = jnp.arange(SLOTS, dtype=jnp.int32)
        live_mask = (slot_index[None, :] < row_counts[:, None]) & (global_row >= 0) & (global_row < FINE)
        safe_row = jnp.clip(global_row, 0, FINE - 1).astype(jnp.int32)
        left_prod = jnp.einsum("ips,isn->ipn", r_rows.astype(jnp.float32), a_rows.astype(jnp.float32))
        left_prod = left_prod.astype(jnp.bfloat16).reshape(ROWS_DEV, BLK, SLOTS, BLK)
        far_blocks = restrict[safe_row.reshape(-1)].reshape(ROWS_DEV, SLOTS, BLK, BLK)
        products = jnp.einsum("ipks,ikqs->ikpq", left_prod.astype(jnp.float32), far_blocks.astype(jnp.float32))
        products = products * live_mask.astype(jnp.float32)[:, :, None, None]
        slot_ids = (row_cols // ROWS_DEV) * AGG_DEV + aggregate[safe_row]
        segment = row_agg[:, None] * WINDOW + slot_ids
        summed = jax.ops.segment_sum(products.reshape(ROWS_DEV * SLOTS, BLK, BLK), segment.reshape(-1).astype(jnp.int32), num_segments=AGG_DEV * WINDOW)
        return summed.reshape(AGG_DEV, WINDOW, BLK, BLK).transpose(0, 2, 1, 3).reshape(AGG_DEV, BLK, WINDOW * BLK)

    blocks_out = lax.map(one_device, jnp.arange(blocks, dtype=jnp.int32))
    return blocks_out.reshape(COARSE, BLK, WINDOW * BLK)
```

```python
import functools

import jax
import jax.numpy as jnp
from jax import lax
from jax.experimental import pallas as pl
from jax.experimental.pallas import tpu as pltpu
from jax.sharding import PartitionSpec as P

BLK = 64
SLOTS = 27
ROWS_DEV = 32
AGG_DEV = 2
Y = 4
NZ = 4
TILES = ROWS_DEV // 2
LTILES = (SLOTS + 1) // 2
PIECE = TILES * 4 + 1
MESH = pl.DeviceIdType.MESH


def gather_kernel(n_rows, with_left, x_ref, a_hbm, g_ref, l_hbm, a_buf, l_buf, send_sem, recv_sem, own_sem, a_sem, l_sem):
    r = lax.axis_index("rows")
    col = lax.axis_index("cols")
    y = col // 2
    zh = lax.rem(col, 2)
    c = lax.rem(r, 2)
    zlo = lax.rem(r // 2, NZ)
    d = 1 - 2 * c
    partner = r + d
    far = r - d
    has_far = jnp.logical_and(far >= 0, far < n_rows)
    turn = jnp.logical_or(
        jnp.logical_and(zlo == 0, c == 0), jnp.logical_and(zlo == NZ - 1, c == 1)
    ).astype(jnp.int32)
    near_z = lax.rem(zh + turn, 2)
    other_z = 1 - near_z
    t3 = jnp.where(has_far, far, r)
    z3 = jnp.where(has_far, other_z, 1 - zh)
    r3_row = jnp.where(has_far, far, partner)
    r3_z = jnp.where(has_far, near_z, zh)

    def ring(step):
        return lax.rem(y + step + 2 * Y, Y)

    yf, yb, y2 = ring(d), ring(-d), ring(2)

    def dev(row, yy, zz):
        return (row, yy * 2 + zz)

    me_near = dev(far, y, near_z)
    me_other = dev(t3, y, z3)
    me_part = dev(partner, y, zh)
    me_yf = dev(r, yf, zh)
    me_yb = dev(r, yb, zh)
    me_r3 = dev(r3_row, y, r3_z)

    def slot(row, slab, yy, zz):
        return (slab - row + 1) * (2 * Y) + yy * 2 + zz

    def copy(src, slab, yy, zz, to, index):
        return pltpu.make_async_remote_copy(
            src_ref=src,
            dst_ref=g_ref.at[slot(to[0], slab, yy, zz)],
            send_sem=send_sem.at[index],
            recv_sem=recv_sem.at[slot(to[0], slab, yy, zz)],
            device_id=to,
            device_id_type=MESH,
        )

    def own_copy(to, index):
        return copy(x_ref, r, y, zh, to, index)

    def relay(slab, yy, zz, to, index):
        return copy(g_ref.at[slot(r, slab, yy, zz)], slab, yy, zz, to, index)

    def arrived(slab, yy, zz):
        s = slot(r, slab, yy, zz)
        pltpu.make_async_remote_copy(
            src_ref=g_ref.at[s],
            dst_ref=g_ref.at[s],
            send_sem=send_sem.at[0],
            recv_sem=recv_sem.at[s],
            device_id=me_part,
            device_id_type=MESH,
        ).wait_recv()

    groups = ROWS_DEV // 4

    def a_copy(k):
        rows = pl.ds(k * 4, 4)
        return pltpu.make_async_copy(a_hbm.at[rows], a_buf.at[rows], a_sem.at[k])

    def l_copy(k):
        rows = pl.ds(k * 4, 4)
        return pltpu.make_async_copy(l_buf.at[rows], l_hbm.at[rows], l_sem.at[k])

    if with_left:

        @pl.loop(0, groups)
        def _(k):
            a_copy(k).start()

    barrier = pltpu.get_barrier_semaphore()
    for to in (me_other, me_part, me_yf, me_yb):
        pl.semaphore_signal(barrier, inc=1, device_id=to, device_id_type=MESH)

    @pl.when(has_far)
    def _():
        pl.semaphore_signal(barrier, inc=1, device_id=me_near, device_id_type=MESH)

    pl.semaphore_wait(barrier, 4 + has_far.astype(jnp.int32))

    @pl.when(has_far)
    def _():
        own_copy(me_near, 1).start()

    own_copy(me_other, 0).start()
    own_copy(me_yf, 2).start()
    own_copy(me_yb, 3).start()
    own_copy(me_part, 4).start()
    mine = pltpu.make_async_copy(x_ref, g_ref.at[slot(r, r, y, zh)], own_sem)
    mine.start()

    if with_left:
        low = lax.broadcasted_iota(jnp.int32, (BLK, 128), 1) < BLK
        zero = jnp.zeros((BLK, 128), jnp.bfloat16)

        @pl.loop(0, groups)
        def _(k):
            a_copy(k).wait()
            t0 = x_ref[pl.ds(k * 8, 4)].reshape(BLK, 128)
            t1 = x_ref[pl.ds(k * 8 + 4, 4)].reshape(BLK, 128)
            left_half = jnp.concatenate(
                [jnp.where(low, t0, zero), jnp.where(low, zero, t0), zero, zero], axis=0
            )
            right_half = jnp.concatenate(
                [zero, zero, jnp.where(low, t1, zero), jnp.where(low, zero, t1)], axis=0
            )
            lhs = jnp.concatenate([left_half, right_half], axis=1)
            rows = pl.ds(k * 4, 4)
            for n in range((SLOTS * BLK + 255) // 256):
                width = min(256, SLOTS * BLK - n * 256)
                rhs = a_buf[rows, :, n * 256 : n * 256 + width].reshape(4 * BLK, width)
                prod = jnp.dot(lhs, rhs, preferred_element_type=jnp.float32).astype(jnp.bfloat16)
                l_buf[rows, 2 * n] = prod[:, :128].reshape(4, BLK, 128)
                l_buf[rows, 2 * n + 1, :, : width - 128] = prod[:, 128:].reshape(4, BLK, width - 128)
            l_copy(k).start()

    arrived(r, yb, zh)
    relay(r, yb, zh, me_yf, 10).start()
    relay(r, yb, zh, me_part, 11).start()
    arrived(r, yf, zh)
    relay(r, yf, zh, me_part, 12).start()

    @pl.when(has_far)
    def _():
        arrived(far, y, near_z)
        relay(far, y, near_z, me_yf, 8).start()
        relay(far, y, near_z, me_yb, 9).start()

    arrived(t3, y, z3)
    relay(t3, y, z3, me_yf, 5).start()
    relay(t3, y, z3, me_yb, 6).start()
    relay(t3, y, z3, me_r3, 7).start()
    arrived(r, y2, zh)
    relay(r, y2, zh, me_part, 17).start()
    arrived(t3, yf, z3)
    relay(t3, yf, z3, me_yb, 13).start()
    relay(t3, yf, z3, me_r3, 15).start()
    arrived(t3, yb, z3)
    relay(t3, yb, z3, me_r3, 14).start()

    @pl.when(has_far)
    def _():
        arrived(r, y, 1 - zh)
        relay(r, y, 1 - zh, me_part, 19).start()
        arrived(far, yb, near_z)
        relay(far, yb, near_z, me_yf, 16).start()

    arrived(t3, y2, z3)
    relay(t3, y2, z3, me_r3, 18).start()

    @pl.when(has_far)
    def _():
        arrived(r, yf, 1 - zh)
        relay(r, yf, 1 - zh, me_part, 20).start()
        arrived(r, yb, 1 - zh)
        relay(r, yb, 1 - zh, me_part, 21).start()
        arrived(r, y2, 1 - zh)
        relay(r, y2, 1 - zh, me_part, 22).start()
        arrived(far, yf, near_z)
        arrived(far, y2, near_z)

    for yy in range(Y):
        for zz in range(2):
            arrived(partner, yy, zz)
    mine.wait()

    own_copy(me_other, 0).wait_send()
    own_copy(me_yf, 2).wait_send()
    own_copy(me_yb, 3).wait_send()
    own_copy(me_part, 4).wait_send()
    relay(t3, y, z3, me_yf, 5).wait_send()
    relay(t3, y, z3, me_yb, 6).wait_send()
    relay(t3, y, z3, me_r3, 7).wait_send()
    relay(r, yb, zh, me_yf, 10).wait_send()
    relay(r, yb, zh, me_part, 11).wait_send()
    relay(r, yf, zh, me_part, 12).wait_send()
    relay(t3, yf, z3, me_yb, 13).wait_send()
    relay(t3, yb, z3, me_r3, 14).wait_send()
    relay(t3, yf, z3, me_r3, 15).wait_send()
    relay(r, y2, zh, me_part, 17).wait_send()
    relay(t3, y2, z3, me_r3, 18).wait_send()

    @pl.when(has_far)
    def _():
        own_copy(me_near, 1).wait_send()
        relay(far, y, near_z, me_yf, 8).wait_send()
        relay(far, y, near_z, me_yb, 9).wait_send()
        relay(far, yb, near_z, me_yf, 16).wait_send()
        relay(r, y, 1 - zh, me_part, 19).wait_send()
        relay(r, yf, 1 - zh, me_part, 20).wait_send()
        relay(r, yb, 1 - zh, me_part, 21).wait_send()
        relay(r, y2, 1 - zh, me_part, 22).wait_send()

    if with_left:

        @pl.loop(0, groups)
        def _(k):
            l_copy(k).wait()


def gather(piece, matrix_blocks, n_rows, with_left=True):
    return pl.pallas_call(
        functools.partial(gather_kernel, n_rows, with_left),
        out_shape=(
            jax.ShapeDtypeStruct((6 * Y,) + piece.shape, piece.dtype),
            jax.ShapeDtypeStruct((ROWS_DEV, LTILES, BLK, 128), jnp.bfloat16),
        ),
        in_specs=[pl.BlockSpec(memory_space=pltpu.VMEM), pl.BlockSpec(memory_space=pl.ANY)],
        out_specs=(pl.BlockSpec(memory_space=pl.ANY), pl.BlockSpec(memory_space=pl.ANY)),
        scratch_shapes=[
            pltpu.VMEM((ROWS_DEV, BLK, SLOTS * BLK), jnp.bfloat16),
            pltpu.VMEM((ROWS_DEV, LTILES, BLK, 128), jnp.bfloat16),
            pltpu.SemaphoreType.DMA((23,)),
            pltpu.SemaphoreType.DMA((6 * Y,)),
            pltpu.SemaphoreType.DMA,
            pltpu.SemaphoreType.DMA((ROWS_DEV // 4,)),
            pltpu.SemaphoreType.DMA((ROWS_DEV // 4,)),
        ],
        compiler_params=pltpu.CompilerParams(
            collective_id=0, has_side_effects=True, vmem_limit_bytes=40 << 20
        ),
        name="gather_left",
    )(piece, matrix_blocks)


def entry_kernel(seg_ref, col_ref, count_ref, g_hbm, l_hbm, out_ref, g_buf, l_buf, acc, g_sem, l_sem):
    window = 6 * Y * AGG_DEV
    lane = lax.broadcasted_iota(jnp.int32, (BLK, 128), 1)
    zero = jnp.zeros((BLK, 128), jnp.bfloat16)

    def g_copy(k):
        return pltpu.make_async_copy(g_hbm.at[k], g_buf.at[k], g_sem.at[k])

    def l_copy(k):
        rows = pl.ds(k * 4, 4)
        return pltpu.make_async_copy(l_hbm.at[rows], l_buf.at[rows], l_sem.at[k])

    @pl.loop(0, 6 * Y)
    def _(k):
        g_copy(k).start()

    @pl.loop(0, ROWS_DEV // 4)
    def _(k):
        l_copy(k).start()

    @pl.loop(0, AGG_DEV * window)
    def _(k):
        acc[k] = jnp.zeros((BLK, BLK), jnp.float32)

    @pl.loop(0, 6 * Y)
    def _(k):
        g_copy(k).wait()

    @pl.loop(0, ROWS_DEV // 4)
    def _(k):
        l_copy(k).wait()

    @pl.loop(0, ROWS_DEV)
    def _(i):
        count = count_ref[i]
        for base in range(0, SLOTS, 4):

            @pl.when(base < count)
            def _():
                prods = []
                for k in range(base, min(base + 4, SLOTS)):
                    col = col_ref[i * SLOTS + k]
                    half = lax.rem(col, 2)
                    dev = col // ROWS_DEV
                    tile = lax.rem(col, ROWS_DEV) // 2
                    right = g_buf[dev, pl.ds(tile * 4, 4)].reshape(BLK, 128)
                    left = l_buf[i, k // 2]
                    if k % 2 == 0:
                        shift = half * BLK
                    else:
                        shift = BLK - half * BLK
                    left = pltpu.roll(left, shift, 1)
                    left = jnp.where((lane >= BLK) == (half == 1), left, zero)
                    prods.append(
                        lax.dot_general(
                            left, right, (((1,), (1,)), ((), ())), preferred_element_type=jnp.float32
                        )
                    )
                for k, prod in zip(range(base, base + 4), prods):
                    seg = seg_ref[i * SLOTS + k]
                    acc[seg] += prod

    for a in range(AGG_DEV):

        @pl.loop(0, window // 2)
        def _(w):
            pair = jnp.concatenate([acc[a * window + 2 * w], acc[a * window + 2 * w + 1]], axis=1)
            out_ref[a, :, pl.ds(pl.multiple_of(w * 128, 128), 128)] = pair


def entries(seg, cols, counts, gathered, left):
    window = 6 * Y * AGG_DEV
    return pl.pallas_call(
        entry_kernel,
        out_shape=jax.ShapeDtypeStruct((AGG_DEV, BLK, window * BLK), jnp.float32),
        in_specs=[pl.BlockSpec(memory_space=pltpu.SMEM)] * 3 + [pl.BlockSpec(memory_space=pl.ANY)] * 2,
        out_specs=pl.BlockSpec(memory_space=pltpu.VMEM),
        scratch_shapes=[
            pltpu.VMEM((6 * Y, PIECE, 16, 128), jnp.bfloat16),
            pltpu.VMEM((ROWS_DEV, LTILES, BLK, 128), jnp.bfloat16),
            pltpu.VMEM((AGG_DEV * window + 1, BLK, BLK), jnp.float32),
            pltpu.SemaphoreType.DMA((6 * Y,)),
            pltpu.SemaphoreType.DMA((ROWS_DEV // 4,)),
        ],
        compiler_params=pltpu.CompilerParams(vmem_limit_bytes=48 << 20),
        name="entries",
    )(seg, cols, counts, gathered, left)


def per_device(matrix_blocks, restrict, columns, counts, aggregate):
    n_rows = lax.axis_size("rows")
    slab_index = lax.axis_index("rows")
    slab_rows = ROWS_DEV * 2 * Y
    window = 6 * Y * AGG_DEV
    tiles = restrict.reshape(TILES, 2, 4, 16, BLK).transpose(0, 2, 3, 1, 4).reshape(TILES * 4, 16, 128)
    agg_tile = jnp.pad(aggregate.astype(jnp.bfloat16)[None, None, :], ((0, 0), (0, 15), (0, 96)))
    piece = jnp.concatenate([tiles, agg_tile], axis=0)
    gathered, left = gather(piece, matrix_blocks, n_rows)
    near_aggs = gathered[:, PIECE - 1, 0, :ROWS_DEV].astype(jnp.int32).reshape(-1)
    inside = ((columns >= slab_rows) | (slab_index > 0)) & (
        (columns < 2 * slab_rows) | (slab_index < n_rows - 1)
    )
    slot_index = jnp.arange(SLOTS, dtype=jnp.int32)
    live = (slot_index[None, :] < counts[:, None]) & inside
    slot_ids = columns // ROWS_DEV * AGG_DEV + near_aggs[columns]
    seg = jnp.where(live, aggregate[:, None] * window + slot_ids, AGG_DEV * window)
    return entries(seg.reshape(-1), columns.reshape(-1), counts, gathered, left)


def solution(mesh):
    return jax.shard_map(
        per_device,
        mesh=mesh,
        in_specs=(
            P(("rows", "cols"), None, None),
            P(("rows", "cols"), None),
            P(("rows", "cols"), None),
            P(("rows", "cols")),
            P(("rows", "cols")),
        ),
        out_specs=P(("rows", "cols"), None, None),
        check_vma=False,
    )
```

```python
import functools

import jax
import jax.numpy as jnp
from jax import lax
from jax.experimental import pallas as pl
from jax.experimental.pallas import tpu as pltpu
from jax.sharding import PartitionSpec as P

BLK = 64
SLOTS = 27
ROWS_DEV = 32
AGG_DEV = 2
Y = 4
NZ = 4
TILES = ROWS_DEV // 2
PIECE = TILES * 4 + 1
MESH = pl.DeviceIdType.MESH


def gather_kernel(n_rows, with_left, x_ref, a_hbm, g_ref, l_hbm, a_buf, l_buf, send_sem, recv_sem, own_sem, a_sem, l_sem):
    r = lax.axis_index("rows")
    col = lax.axis_index("cols")
    y = col // 2
    zh = lax.rem(col, 2)
    c = lax.rem(r, 2)
    zlo = lax.rem(r // 2, NZ)
    d = 1 - 2 * c
    partner = r + d
    far = r - d
    has_far = jnp.logical_and(far >= 0, far < n_rows)
    turn = jnp.logical_or(
        jnp.logical_and(zlo == 0, c == 0), jnp.logical_and(zlo == NZ - 1, c == 1)
    ).astype(jnp.int32)
    near_z = lax.rem(zh + turn, 2)
    other_z = 1 - near_z
    t3 = jnp.where(has_far, far, r)
    z3 = jnp.where(has_far, other_z, 1 - zh)
    r3_row = jnp.where(has_far, far, partner)
    r3_z = jnp.where(has_far, near_z, zh)

    def ring(step):
        return lax.rem(y + step + 2 * Y, Y)

    yf, yb, y2 = ring(d), ring(-d), ring(2)

    def dev(row, yy, zz):
        return (row, yy * 2 + zz)

    me_near = dev(far, y, near_z)
    me_other = dev(t3, y, z3)
    me_part = dev(partner, y, zh)
    me_yf = dev(r, yf, zh)
    me_yb = dev(r, yb, zh)
    me_r3 = dev(r3_row, y, r3_z)

    def slot(row, slab, yy, zz):
        return (slab - row + 1) * (2 * Y) + yy * 2 + zz

    def copy(src, slab, yy, zz, to, index):
        return pltpu.make_async_remote_copy(
            src_ref=src,
            dst_ref=g_ref.at[slot(to[0], slab, yy, zz)],
            send_sem=send_sem.at[index],
            recv_sem=recv_sem.at[slot(to[0], slab, yy, zz)],
            device_id=to,
            device_id_type=MESH,
        )

    def own_copy(to, index):
        return copy(x_ref, r, y, zh, to, index)

    def relay(slab, yy, zz, to, index):
        return copy(g_ref.at[slot(r, slab, yy, zz)], slab, yy, zz, to, index)

    def arrived(slab, yy, zz):
        s = slot(r, slab, yy, zz)
        pltpu.make_async_remote_copy(
            src_ref=g_ref.at[s],
            dst_ref=g_ref.at[s],
            send_sem=send_sem.at[0],
            recv_sem=recv_sem.at[s],
            device_id=me_part,
            device_id_type=MESH,
        ).wait_recv()

    groups = ROWS_DEV // 4

    def a_copy(k):
        rows = pl.ds(k * 4, 4)
        return pltpu.make_async_copy(a_hbm.at[rows], a_buf.at[rows], a_sem.at[k])

    def l_copy(k):
        rows = pl.ds(k * 4, 4)
        return pltpu.make_async_copy(l_buf.at[rows], l_hbm.at[rows], l_sem.at[k])

    if with_left:

        @pl.loop(0, groups)
        def _(k):
            a_copy(k).start()

    barrier = pltpu.get_barrier_semaphore()
    for to in (me_other, me_part, me_yf, me_yb):
        pl.semaphore_signal(barrier, inc=1, device_id=to, device_id_type=MESH)

    @pl.when(has_far)
    def _():
        pl.semaphore_signal(barrier, inc=1, device_id=me_near, device_id_type=MESH)

    pl.semaphore_wait(barrier, 4 + has_far.astype(jnp.int32))

    @pl.when(has_far)
    def _():
        own_copy(me_near, 1).start()

    own_copy(me_other, 0).start()
    own_copy(me_yf, 2).start()
    own_copy(me_yb, 3).start()
    own_copy(me_part, 4).start()
    mine = pltpu.make_async_copy(x_ref, g_ref.at[slot(r, r, y, zh)], own_sem)
    mine.start()

    if with_left:
        low = lax.broadcasted_iota(jnp.int32, (BLK, 128), 1) < BLK
        zero = jnp.zeros((BLK, 128), jnp.bfloat16)

        @pl.loop(0, groups)
        def _(k):
            a_copy(k).wait()
            t0 = x_ref[pl.ds(k * 8, 4)].reshape(BLK, 128)
            t1 = x_ref[pl.ds(k * 8 + 4, 4)].reshape(BLK, 128)
            left_half = jnp.concatenate(
                [jnp.where(low, t0, zero), jnp.where(low, zero, t0), zero, zero], axis=0
            )
            right_half = jnp.concatenate(
                [zero, zero, jnp.where(low, t1, zero), jnp.where(low, zero, t1)], axis=0
            )
            lhs = jnp.concatenate([left_half, right_half], axis=1)
            rows = pl.ds(k * 4, 4)
            for n in range((SLOTS * BLK + 255) // 256):
                width = min(256, SLOTS * BLK - n * 256)
                rhs = a_buf[rows, :, n * 256 : n * 256 + width].reshape(4 * BLK, width)
                prod = lax.dot_general(
                    lhs, rhs, (((0,), (0,)), ((), ())), preferred_element_type=jnp.float32
                ).astype(jnp.bfloat16)
                for s in range(width // BLK):
                    l_buf[rows, 4 * n + s] = prod[:, s * BLK : (s + 1) * BLK].reshape(4, BLK, BLK)
            l_copy(k).start()

    arrived(r, yb, zh)
    relay(r, yb, zh, me_yf, 10).start()
    relay(r, yb, zh, me_part, 11).start()
    arrived(r, yf, zh)
    relay(r, yf, zh, me_part, 12).start()

    @pl.when(has_far)
    def _():
        arrived(far, y, near_z)
        relay(far, y, near_z, me_yf, 8).start()
        relay(far, y, near_z, me_yb, 9).start()

    arrived(t3, y, z3)
    relay(t3, y, z3, me_yf, 5).start()
    relay(t3, y, z3, me_yb, 6).start()
    relay(t3, y, z3, me_r3, 7).start()
    arrived(r, y2, zh)
    relay(r, y2, zh, me_part, 17).start()
    arrived(t3, yf, z3)
    relay(t3, yf, z3, me_yb, 13).start()
    relay(t3, yf, z3, me_r3, 15).start()
    arrived(t3, yb, z3)
    relay(t3, yb, z3, me_r3, 14).start()

    @pl.when(has_far)
    def _():
        arrived(r, y, 1 - zh)
        relay(r, y, 1 - zh, me_part, 19).start()
        arrived(far, yb, near_z)
        relay(far, yb, near_z, me_yf, 16).start()

    arrived(t3, y2, z3)
    relay(t3, y2, z3, me_r3, 18).start()

    @pl.when(has_far)
    def _():
        arrived(r, yf, 1 - zh)
        relay(r, yf, 1 - zh, me_part, 20).start()
        arrived(r, yb, 1 - zh)
        relay(r, yb, 1 - zh, me_part, 21).start()
        arrived(r, y2, 1 - zh)
        relay(r, y2, 1 - zh, me_part, 22).start()
        arrived(far, yf, near_z)
        arrived(far, y2, near_z)

    for yy in range(Y):
        for zz in range(2):
            arrived(partner, yy, zz)
    mine.wait()

    own_copy(me_other, 0).wait_send()
    own_copy(me_yf, 2).wait_send()
    own_copy(me_yb, 3).wait_send()
    own_copy(me_part, 4).wait_send()
    relay(t3, y, z3, me_yf, 5).wait_send()
    relay(t3, y, z3, me_yb, 6).wait_send()
    relay(t3, y, z3, me_r3, 7).wait_send()
    relay(r, yb, zh, me_yf, 10).wait_send()
    relay(r, yb, zh, me_part, 11).wait_send()
    relay(r, yf, zh, me_part, 12).wait_send()
    relay(t3, yf, z3, me_yb, 13).wait_send()
    relay(t3, yb, z3, me_r3, 14).wait_send()
    relay(t3, yf, z3, me_r3, 15).wait_send()
    relay(r, y2, zh, me_part, 17).wait_send()
    relay(t3, y2, z3, me_r3, 18).wait_send()

    @pl.when(has_far)
    def _():
        own_copy(me_near, 1).wait_send()
        relay(far, y, near_z, me_yf, 8).wait_send()
        relay(far, y, near_z, me_yb, 9).wait_send()
        relay(far, yb, near_z, me_yf, 16).wait_send()
        relay(r, y, 1 - zh, me_part, 19).wait_send()
        relay(r, yf, 1 - zh, me_part, 20).wait_send()
        relay(r, yb, 1 - zh, me_part, 21).wait_send()
        relay(r, y2, 1 - zh, me_part, 22).wait_send()

    if with_left:

        @pl.loop(0, groups)
        def _(k):
            l_copy(k).wait()


def gather(piece, matrix_blocks, n_rows, with_left=True):
    return pl.pallas_call(
        functools.partial(gather_kernel, n_rows, with_left),
        out_shape=(
            pltpu.HBM((6 * Y,) + piece.shape, piece.dtype),
            pltpu.HBM((ROWS_DEV, SLOTS, BLK, BLK), jnp.bfloat16),
        ),
        in_specs=[pl.BlockSpec(memory_space=pltpu.VMEM), pl.BlockSpec(memory_space=pltpu.HBM)],
        out_specs=(pl.BlockSpec(memory_space=pltpu.HBM), pl.BlockSpec(memory_space=pltpu.HBM)),
        scratch_shapes=[
            pltpu.VMEM((ROWS_DEV, BLK, SLOTS * BLK), jnp.bfloat16),
            pltpu.VMEM((ROWS_DEV, SLOTS, BLK, BLK), jnp.bfloat16),
            pltpu.SemaphoreType.DMA((23,)),
            pltpu.SemaphoreType.DMA((6 * Y,)),
            pltpu.SemaphoreType.DMA,
            pltpu.SemaphoreType.DMA((ROWS_DEV // 4,)),
            pltpu.SemaphoreType.DMA((ROWS_DEV // 4,)),
        ],
        compiler_params=pltpu.CompilerParams(
            collective_id=0, has_side_effects=True, vmem_limit_bytes=32 << 20
        ),
        name="gather_left",
    )(piece, pltpu.with_memory_space_constraint(matrix_blocks, pltpu.HBM))


def entry_kernel(chunk, n_rows, agg_ref, col_ref, count_ref, own_ref, slab_ref, g_hbm, l_hbm, out_ref, g_ref, l_ref, acc, g_sem, l_sem):
    n_dev = 6 * Y
    trash = 2 * AGG_DEV * n_dev
    half = lax.broadcasted_iota(jnp.int32, (BLK, 128), 1) // BLK
    slab = slab_ref[0]
    first = jnp.where(slab > 0, 0, ROWS_DEV * 2 * Y)
    last = jnp.where(slab < n_rows - 1, ROWS_DEV * 6 * Y, ROWS_DEV * 4 * Y)

    def g_copy(k):
        return pltpu.make_async_copy(g_hbm.at[k], g_ref.at[k], g_sem.at[k])

    def l_copy(k):
        rows = pl.ds(k * 4, 4)
        return pltpu.make_async_copy(l_hbm.at[rows], l_ref.at[rows], l_sem.at[k])

    @pl.loop(0, n_dev)
    def _(k):
        g_copy(k).start()

    @pl.loop(0, ROWS_DEV // 4)
    def _(k):
        l_copy(k).start()

    @pl.loop(0, trash)
    def _(k):
        acc[k] = jnp.zeros((BLK, 128), jnp.float32)

    @pl.loop(0, n_dev)
    def _(k):
        g_copy(k).wait()

    @pl.loop(0, ROWS_DEV)
    def _(i):
        @pl.when(lax.rem(i, 4) == 0)
        def _():
            l_copy(i // 4).wait()

        count = count_ref[i]
        own = own_ref[i] * (2 * n_dev)
        for base in range(0, SLOTS, chunk):

            @pl.when(base < count)
            def _():
                prods = []
                for k in range(base, min(base + chunk, SLOTS)):
                    col = col_ref[i, k]
                    dev = col // ROWS_DEV
                    tile = lax.rem(col, ROWS_DEV) // 2
                    side = lax.rem(col, 2)
                    live = (k < count) & (col >= first) & (col < last)
                    right = g_ref[dev, pl.ds(tile * 4, 4)].reshape(BLK, 128)
                    prod = jnp.dot(l_ref[i, k], right, preferred_element_type=jnp.float32)
                    crossed = (agg_ref[col] != side).astype(jnp.int32)
                    seg = jnp.where(live, own + dev * 2 + crossed, trash)
                    prods.append((seg, side, prod))
                for seg, side, prod in prods:
                    acc[seg] += jnp.where(half == side, prod, 0.0)

    for a in range(AGG_DEV):

        @pl.loop(0, n_dev)
        def _(w):
            s = (a * n_dev + w) * 2
            pair = acc[s] + pltpu.roll(acc[s + 1], BLK, 1)
            out_ref[a, :, pl.ds(pl.multiple_of(w * 128, 128), 128)] = pair


def entries(aggs, cols, counts, own, slab, gathered, left, n_rows, chunk=7):
    n_dev = 6 * Y
    return pl.pallas_call(
        functools.partial(entry_kernel, chunk, n_rows),
        out_shape=jax.ShapeDtypeStruct((AGG_DEV, BLK, n_dev * AGG_DEV * BLK), jnp.float32),
        in_specs=[pl.BlockSpec(memory_space=pltpu.SMEM)] * 5 + [pl.BlockSpec(memory_space=pltpu.HBM)] * 2,
        out_specs=pl.BlockSpec(memory_space=pltpu.VMEM),
        scratch_shapes=[
            pltpu.VMEM((n_dev, PIECE, 16, 128), jnp.bfloat16),
            pltpu.VMEM((ROWS_DEV, SLOTS, BLK, BLK), jnp.bfloat16),
            pltpu.VMEM((2 * AGG_DEV * n_dev + 1, BLK, 128), jnp.float32),
            pltpu.SemaphoreType.DMA((n_dev,)),
            pltpu.SemaphoreType.DMA((ROWS_DEV // 4,)),
        ],
        compiler_params=pltpu.CompilerParams(vmem_limit_bytes=40 << 20),
        name="entries",
    )(
        aggs,
        cols,
        counts,
        own,
        slab,
        pltpu.with_memory_space_constraint(gathered, pltpu.HBM),
        pltpu.with_memory_space_constraint(left, pltpu.HBM),
    )


def per_device(matrix_blocks, restrict, columns, counts, aggregate):
    n_rows = lax.axis_size("rows")
    slab = lax.axis_index("rows").astype(jnp.int32).reshape(1)
    tiles = restrict.reshape(TILES, 2, BLK, BLK).transpose(0, 3, 1, 2).reshape(TILES * 4, 16, 128)
    agg_tile = jnp.pad(aggregate.astype(jnp.bfloat16)[None, None, :], ((0, 0), (0, 15), (0, 96)))
    piece = jnp.concatenate([tiles, agg_tile], axis=0)
    gathered, left = gather(piece, matrix_blocks, n_rows)
    near_aggs = gathered[:, PIECE - 1, 0, :ROWS_DEV].astype(jnp.int32).reshape(-1)
    return entries(near_aggs, columns, counts, aggregate, slab, gathered, left, n_rows)


def solution(mesh):
    return jax.shard_map(
        per_device,
        mesh=mesh,
        in_specs=(
            P(("rows", "cols"), None, None),
            P(("rows", "cols"), None),
            P(("rows", "cols"), None),
            P(("rows", "cols")),
            P(("rows", "cols")),
        ),
        out_specs=P(("rows", "cols"), None, None),
        check_vma=False,
    )
```

```python
import functools

import jax
import jax.numpy as jnp
from jax import lax
from jax.experimental import pallas as pl
from jax.experimental.pallas import tpu as pltpu
from jax.sharding import PartitionSpec as P

BLK = 64
SLOTS = 27
ROWS_DEV = 32
AGG_DEV = 2
Y = 4
NZ = 4
TILES = ROWS_DEV // 2
PIECE = TILES * 4 + 1
PAIRS = (SLOTS + 1) // 2
MESH = pl.DeviceIdType.MESH
ORDER = {
    "own_b": 4, "own_f": 5, "near_0": 8, "other_0": 10, "own_2": 12, "other_f": 17, "near_b": 17.5, "other_b": 18,
    "other_2": 22, "back_0": 24, "back_f": 27, "near_f": 27.5, "back_b": 28, "near_2": 28.5, "back_2": 31,
}


def gather_kernel(n_rows, with_left, chunks, pace, x_ref, a_hbm, g_ref, l_hbm, a_buf, l_buf, send_sem, recv_sem, own_sem, a_sem, l_sem):
    r = lax.axis_index("rows")
    col = lax.axis_index("cols")
    y = col // 2
    zh = lax.rem(col, 2)
    c = lax.rem(r, 2)
    zlo = lax.rem(r // 2, NZ)
    d = 1 - 2 * c
    partner = r + d
    far = r - d
    has_far = jnp.logical_and(far >= 0, far < n_rows)
    turn = jnp.logical_or(
        jnp.logical_and(zlo == 0, c == 0), jnp.logical_and(zlo == NZ - 1, c == 1)
    ).astype(jnp.int32)
    near_z = lax.rem(zh + turn, 2)
    other_z = 1 - near_z
    t3 = jnp.where(has_far, far, r)
    z3 = jnp.where(has_far, other_z, 1 - zh)
    r3_row = jnp.where(has_far, far, partner)
    r3_z = jnp.where(has_far, near_z, zh)

    def ring(step):
        return lax.rem(y + step + 2 * Y, Y)

    yf, yb, y2 = ring(d), ring(-d), ring(2)

    def dev(row, yy, zz):
        return (row, yy * 2 + zz)

    me_near = dev(far, y, near_z)
    me_other = dev(t3, y, z3)
    me_part = dev(partner, y, zh)
    me_yf = dev(r, yf, zh)
    me_yb = dev(r, yb, zh)
    me_r3 = dev(r3_row, y, r3_z)

    def slot(row, slab, yy, zz):
        return (slab - row + 1) * (2 * Y) + yy * 2 + zz

    size = x_ref.shape[0]
    cuts = [size // chunks * k for k in range(chunks)] + [size]

    def copy(src, slab, yy, zz, to, index, part):
        span = pl.ds(cuts[part], cuts[part + 1] - cuts[part])
        to_slot = slot(to[0], slab, yy, zz)
        return pltpu.make_async_remote_copy(
            src_ref=src.at[span],
            dst_ref=g_ref.at[to_slot, span],
            send_sem=send_sem.at[index, part],
            recv_sem=recv_sem.at[to_slot, part],
            device_id=to,
            device_id_type=MESH,
        )

    def own_copy(to, index, part):
        return copy(x_ref, r, y, zh, to, index, part)

    def relay(slab, yy, zz, to, index, part):
        return copy(g_ref.at[slot(r, slab, yy, zz)], slab, yy, zz, to, index, part)

    def arrived(slab, yy, zz, part):
        span = pl.ds(cuts[part], cuts[part + 1] - cuts[part])
        s = slot(r, slab, yy, zz)
        pltpu.make_async_remote_copy(
            src_ref=g_ref.at[s, span],
            dst_ref=g_ref.at[s, span],
            send_sem=send_sem.at[0, part],
            recv_sem=recv_sem.at[s, part],
            device_id=me_part,
            device_id_type=MESH,
        ).wait_recv()

    own_piece, far_near, far_other, own_other = (r, zh), (far, near_z), (t3, z3), (r, 1 - zh)
    stages = {
        "own_b": (own_piece, yb, False, [(me_yf, 10), (me_part, 11)]),
        "own_f": (own_piece, yf, False, [(me_part, 12)]),
        "own_2": (own_piece, y2, False, [(me_part, 17)]),
        "near_0": (far_near, y, True, [(me_yf, 8), (me_yb, 9)]),
        "near_b": (far_near, yb, True, [(me_yf, 16)]),
        "near_f": (far_near, yf, True, []),
        "near_2": (far_near, y2, True, []),
        "other_0": (far_other, y, False, [(me_yf, 5), (me_yb, 6), (me_r3, 7)]),
        "other_f": (far_other, yf, False, [(me_yb, 13), (me_r3, 15)]),
        "other_b": (far_other, yb, False, [(me_r3, 14)]),
        "other_2": (far_other, y2, False, [(me_r3, 18)]),
        "back_0": (own_other, y, True, [(me_part, 19)]),
        "back_f": (own_other, yf, True, [(me_part, 20)]),
        "back_b": (own_other, yb, True, [(me_part, 21)]),
        "back_2": (own_other, y2, True, [(me_part, 22)]),
    }

    def step(name, part):
        (slab, zz), yy, needs_far, targets = stages[name]

        def run():
            arrived(slab, yy, zz, part)
            for to, index in targets:
                relay(slab, yy, zz, to, index, part).start()

        if needs_far:
            pl.when(has_far)(run)
        else:
            run()

    def sent(name, part):
        (slab, zz), yy, needs_far, targets = stages[name]

        def run():
            for to, index in targets:
                relay(slab, yy, zz, to, index, part).wait_send()

        if needs_far:
            pl.when(has_far)(run)
        else:
            run()

    groups = ROWS_DEV // 4

    def a_copy(k):
        rows = pl.ds(k * 4, 4)
        return pltpu.make_async_copy(a_hbm.at[rows], a_buf.at[rows], a_sem.at[k])

    def l_copy(k):
        rows = pl.ds(k * 4, 4)
        return pltpu.make_async_copy(l_buf.at[rows], l_hbm.at[rows], l_sem.at[k])

    if with_left:

        @pl.loop(0, groups)
        def _(k):
            a_copy(k).start()

    barrier = pltpu.get_barrier_semaphore()
    for to in (me_other, me_part, me_yf, me_yb):
        pl.semaphore_signal(barrier, inc=1, device_id=to, device_id_type=MESH)

    @pl.when(has_far)
    def _():
        pl.semaphore_signal(barrier, inc=1, device_id=me_near, device_id_type=MESH)

    pl.semaphore_wait(barrier, 4 + has_far.astype(jnp.int32))

    for part in range(chunks):
        @pl.when(has_far)
        def _(part=part):
            own_copy(me_near, 1, part).start()

        own_copy(me_other, 0, part).start()
        own_copy(me_yf, 2, part).start()
        own_copy(me_yb, 3, part).start()
        own_copy(me_part, 4, part).start()

    mine = pltpu.make_async_copy(x_ref, g_ref.at[slot(r, r, y, zh)], own_sem)
    mine.start()

    if with_left:
        low = lax.broadcasted_iota(jnp.int32, (BLK, 128), 1) < BLK
        zero = jnp.zeros((BLK, 128), jnp.bfloat16)

        @pl.loop(0, groups)
        def _(k):
            a_copy(k).wait()
            t0 = x_ref[pl.ds(k * 8, 4)].reshape(BLK, 128)
            t1 = x_ref[pl.ds(k * 8 + 4, 4)].reshape(BLK, 128)
            left_half = jnp.concatenate(
                [jnp.where(low, t0, zero), jnp.where(low, zero, t0), zero, zero], axis=0
            )
            right_half = jnp.concatenate(
                [zero, zero, jnp.where(low, t1, zero), jnp.where(low, zero, t1)], axis=0
            )
            lhs = jnp.concatenate([left_half, right_half], axis=1)
            rows = pl.ds(k * 4, 4)
            for n in range((SLOTS * BLK + 255) // 256):
                width = min(256, SLOTS * BLK - n * 256)
                rhs = a_buf[rows, :, n * 256 : n * 256 + width].reshape(4 * BLK, width)
                prod = lax.dot_general(
                    lhs, rhs, (((0,), (0,)), ((), ())), preferred_element_type=jnp.float32
                ).astype(jnp.bfloat16)
                l_buf[rows, 2 * n] = prod[:, :128].reshape(4, BLK, 128)
                l_buf[rows, 2 * n + 1, :, : width - 128] = prod[:, 128:].reshape(4, BLK, width - 128)
            l_copy(k).start()

    order = sorted((ORDER[name] + part * pace, name, part) for name in stages for part in range(chunks))
    for _, name, part in order:
        step(name, part)

    for yy in range(Y):
        for zz in range(2):
            for part in range(chunks):
                arrived(partner, yy, zz, part)
    mine.wait()

    for part in range(chunks):
        for to, index in ((me_other, 0), (me_yf, 2), (me_yb, 3), (me_part, 4)):
            own_copy(to, index, part).wait_send()

        @pl.when(has_far)
        def _(part=part):
            own_copy(me_near, 1, part).wait_send()

        for name in stages:
            sent(name, part)

    if with_left:

        @pl.loop(0, groups)
        def _(k):
            l_copy(k).wait()


def gather(piece, matrix_blocks, n_rows, with_left=True, chunks=4, pace=2):
    return pl.pallas_call(
        functools.partial(gather_kernel, n_rows, with_left, chunks, pace),
        out_shape=(
            pltpu.HBM((6 * Y,) + piece.shape, piece.dtype),
            pltpu.HBM((ROWS_DEV, PAIRS, BLK, 128), jnp.bfloat16),
        ),
        in_specs=[pl.BlockSpec(memory_space=pltpu.VMEM), pl.BlockSpec(memory_space=pltpu.HBM)],
        out_specs=(pl.BlockSpec(memory_space=pltpu.HBM), pl.BlockSpec(memory_space=pltpu.HBM)),
        scratch_shapes=[
            pltpu.VMEM((ROWS_DEV, BLK, SLOTS * BLK), jnp.bfloat16),
            pltpu.VMEM((ROWS_DEV, PAIRS, BLK, 128), jnp.bfloat16),
            pltpu.SemaphoreType.DMA((23, chunks)),
            pltpu.SemaphoreType.DMA((6 * Y, chunks)),
            pltpu.SemaphoreType.DMA,
            pltpu.SemaphoreType.DMA((ROWS_DEV // 4,)),
            pltpu.SemaphoreType.DMA((ROWS_DEV // 4,)),
        ],
        compiler_params=pltpu.CompilerParams(
            collective_id=0, has_side_effects=True, vmem_limit_bytes=32 << 20
        ),
        name="gather_left",
    )(piece, pltpu.with_memory_space_constraint(matrix_blocks, pltpu.HBM))


def entry_kernel(unroll, n_rows, own_ref, count_ref, slab_ref, col_ref, g_hbm, l_hbm, out_ref, g_ref, agg_ref, l_ref, acc, tab, words, g_sem, agg_sem, l_sem, tab_sem):
    n_dev = 6 * Y
    trash = 2 * AGG_DEV * n_dev
    half = lax.broadcasted_iota(jnp.int32, (BLK, 128), 1) // BLK
    slab = slab_ref[0]
    first = jnp.where(slab > 0, 0, ROWS_DEV * 2 * Y)
    last = jnp.where(slab < n_rows - 1, ROWS_DEV * 6 * Y, ROWS_DEV * 4 * Y)
    groups = ROWS_DEV * PAIRS // 64

    def agg_copy(k):
        return pltpu.make_async_copy(g_hbm.at[k, PIECE - 1], agg_ref.at[k], agg_sem.at[k])

    def g_copy(k):
        return pltpu.make_async_copy(
            g_hbm.at[k, pl.ds(0, PIECE - 1)], g_ref.at[pl.ds(k * (PIECE - 1), PIECE - 1)], g_sem.at[k]
        )

    def l_copy(k):
        span = pl.ds(k * 64, 64)
        return pltpu.make_async_copy(l_hbm.at[span], l_ref.at[span], l_sem.at[k])

    @pl.loop(0, n_dev)
    def _(k):
        agg_copy(k).start()

    @pl.loop(0, n_dev)
    def _(k):
        g_copy(k).start()

    @pl.loop(0, groups)
    def _(k):
        l_copy(k).start()

    lane = lax.broadcasted_iota(jnp.int32, (1, 128), 1)
    spot = lax.broadcasted_iota(jnp.int32, (8, 128), 0) * 128 + lax.broadcasted_iota(jnp.int32, (8, 128), 1)
    cols = jnp.zeros((8, 128), jnp.int32)
    meta = jnp.zeros((8, 128), jnp.int32)
    total = 0
    for i in range(ROWS_DEV):
        begin = total
        total = total + count_ref[i]
        row = jnp.concatenate([col_ref[pl.ds(i, 1), :], jnp.zeros((1, 128 - SLOTS), jnp.int32)], axis=1)
        row = jnp.broadcast_to(pltpu.roll(row, begin & 127, 1), (8, 128))
        here = (spot >= begin) & (spot < total)
        cols = jnp.where(here, row, cols)
        meta = jnp.where(here, (begin << 6) + (own_ref[i] << 5) + i, meta)
    used = spot < total
    slots = spot - (meta >> 6)
    side = cols & 1

    @pl.loop(0, n_dev)
    def _(k):
        agg_copy(k).wait()

    aggs = jnp.zeros((8, 128), jnp.int32)
    for k in range(n_dev // 4):
        row = jnp.zeros((1, 128), jnp.int32)
        for q in range(4):
            tile = agg_ref[4 * k + q].astype(jnp.float32)[:1].astype(jnp.int32)
            row = row + jnp.where(lane // 32 == q, tile & 1, 0)
        row = jnp.broadcast_to(row, (8, 128))
        got = jnp.take_along_axis(row, cols & 127, axis=1, mode="promise_in_bounds")
        aggs = jnp.where(cols >> 7 == k, got, aggs)
    seg = ((meta >> 5) & 1) * (2 * n_dev) + (cols >> 5) * 2 + (aggs ^ side)
    tab[pl.ds(0, 8), :] = jnp.where(used & (cols >= first) & (cols < last), seg, trash)
    tab[pl.ds(8, 8), :] = cols >> 1
    tab[pl.ds(16, 8), :] = jnp.where(used, (meta & 31) * PAIRS + (slots >> 1), ROWS_DEV * PAIRS - 1)
    tab[pl.ds(24, 8), :] = (slots & 1) * BLK
    tab[pl.ds(32, 8), :] = side
    to_words = pltpu.make_async_copy(tab, words, tab_sem)
    to_words.start()

    @pl.loop(0, trash)
    def _(k):
        acc[k] = jnp.zeros((BLK, 128), jnp.float32)

    to_words.wait()

    @pl.loop(0, n_dev)
    def _(k):
        g_copy(k).wait()

    def body(c, ready):
        base = c * unroll
        r0 = base >> 7
        c0 = base & 127
        need = (words[16 + r0, c0 + unroll - 1] >> 6) + 1

        @pl.loop(ready, need)
        def _(k):
            l_copy(k).wait()

        prods = []
        for u in range(unroll):
            right = g_ref[pl.ds(words[8 + r0, c0 + u] * 4, 4)].reshape(BLK, 128)
            left = pltpu.roll(l_ref[words[16 + r0, c0 + u]], words[24 + r0, c0 + u], 1)[:, :BLK]
            prods.append(jnp.dot(left, right, preferred_element_type=jnp.float32))
        for u, prod in enumerate(prods):
            acc[words[r0, c0 + u]] += jnp.where(half == words[32 + r0, c0 + u], prod, 0.0)
        return jnp.maximum(ready, need)

    ready = lax.fori_loop(0, (total + unroll - 1) // unroll, body, 0)

    @pl.loop(ready, groups)
    def _(k):
        l_copy(k).wait()

    for a in range(AGG_DEV):

        @pl.loop(0, n_dev, unroll=6)
        def _(w):
            s = (a * n_dev + w) * 2
            pair = acc[s] + pltpu.roll(acc[s + 1], BLK, 1)
            out_ref[a, :, pl.ds(pl.multiple_of(w * 128, 128), 128)] = pair


def entries(cols, counts, own, slab, gathered, left, n_rows, chunk=64):
    n_dev = 6 * Y
    return pl.pallas_call(
        functools.partial(entry_kernel, chunk, n_rows),
        out_shape=jax.ShapeDtypeStruct((AGG_DEV, BLK, n_dev * AGG_DEV * BLK), jnp.float32),
        in_specs=[pl.BlockSpec(memory_space=pltpu.SMEM)] * 3
        + [pl.BlockSpec(memory_space=pltpu.VMEM)]
        + [pl.BlockSpec(memory_space=pltpu.HBM)] * 2,
        out_specs=pl.BlockSpec(memory_space=pltpu.VMEM),
        scratch_shapes=[
            pltpu.VMEM((n_dev * (PIECE - 1), 16, 128), jnp.bfloat16),
            pltpu.VMEM((n_dev, 16, 128), jnp.bfloat16),
            pltpu.VMEM((ROWS_DEV * PAIRS, BLK, 128), jnp.bfloat16),
            pltpu.VMEM((2 * AGG_DEV * n_dev + 1, BLK, 128), jnp.float32),
            pltpu.VMEM((40, 128), jnp.int32),
            pltpu.SMEM((40, 128), jnp.int32),
            pltpu.SemaphoreType.DMA((n_dev,)),
            pltpu.SemaphoreType.DMA((n_dev,)),
            pltpu.SemaphoreType.DMA((ROWS_DEV * PAIRS // 64,)),
            pltpu.SemaphoreType.DMA,
        ],
        compiler_params=pltpu.CompilerParams(vmem_limit_bytes=44 << 20),
        name="entries",
    )(
        own,
        counts,
        slab,
        cols,
        pltpu.with_memory_space_constraint(gathered, pltpu.HBM),
        pltpu.with_memory_space_constraint(left.reshape(ROWS_DEV * PAIRS, BLK, 128), pltpu.HBM),
    )


def per_device(matrix_blocks, restrict, columns, counts, aggregate):
    n_rows = lax.axis_size("rows")
    slab = lax.axis_index("rows").astype(jnp.int32).reshape(1)
    tiles = restrict.reshape(TILES, 2, BLK, BLK).transpose(0, 3, 1, 2).reshape(TILES * 4, 16, 128)
    agg_tile = jnp.broadcast_to(aggregate.astype(jnp.bfloat16)[None, None, None, :], (1, 16, 4, ROWS_DEV))
    agg_tile = agg_tile.reshape(1, 16, 128)
    piece = jnp.concatenate([tiles, agg_tile], axis=0)
    gathered, left = gather(piece, matrix_blocks, n_rows)
    return entries(columns, counts, aggregate, slab, gathered, left, n_rows)


def solution(mesh):
    return jax.shard_map(
        per_device,
        mesh=mesh,
        in_specs=(
            P(("rows", "cols"), None, None),
            P(("rows", "cols"), None),
            P(("rows", "cols"), None),
            P(("rows", "cols")),
            P(("rows", "cols")),
        ),
        out_specs=P(("rows", "cols"), None, None),
        check_vma=False,
    )
```

```python
import functools

import jax
import jax.numpy as jnp
from jax import lax
from jax.experimental import pallas as pl
from jax.experimental.pallas import tpu as pltpu
from jax.sharding import PartitionSpec as P

BLK = 64
SLOTS = 27
ROWS_DEV = 32
AGG_DEV = 2
Y = 4
NZ = 4
TILES = ROWS_DEV // 2
PIECE = TILES * 4 + 1
PAIRS = (SLOTS + 1) // 2
MESH = pl.DeviceIdType.MESH
ORDER = {
    "own_b": 1.7, "own_f": 5, "other_0": 7.4, "near_0": 9, "own_2": 12, "other_f": 12.3, "other_b": 18, "near_b": 21.2,
    "back_b": 21.4, "other_2": 22, "back_0": 24, "near_2": 28.5, "back_f": 29.3, "back_2": 34.1, "near_f": 34.4,
}


def gather_kernel(n_rows, with_left, chunks, pace, x_ref, a_hbm, g_ref, l_hbm, a_buf, l_buf, send_sem, recv_sem, own_sem, a_sem, l_sem):
    r = lax.axis_index("rows")
    col = lax.axis_index("cols")
    y = col // 2
    zh = lax.rem(col, 2)
    c = lax.rem(r, 2)
    zlo = lax.rem(r // 2, NZ)
    d = 1 - 2 * c
    partner = r + d
    far = r - d
    has_far = jnp.logical_and(far >= 0, far < n_rows)
    turn = jnp.logical_or(
        jnp.logical_and(zlo == 0, c == 0), jnp.logical_and(zlo == NZ - 1, c == 1)
    ).astype(jnp.int32)
    near_z = lax.rem(zh + turn, 2)
    other_z = 1 - near_z
    t3 = jnp.where(has_far, far, r)
    z3 = jnp.where(has_far, other_z, 1 - zh)
    r3_row = jnp.where(has_far, far, partner)
    r3_z = jnp.where(has_far, near_z, zh)

    def ring(step):
        return lax.rem(y + step + 2 * Y, Y)

    yf, yb, y2 = ring(d), ring(-d), ring(2)

    def dev(row, yy, zz):
        return (row, yy * 2 + zz)

    me_near = dev(far, y, near_z)
    me_other = dev(t3, y, z3)
    me_part = dev(partner, y, zh)
    me_yf = dev(r, yf, zh)
    me_yb = dev(r, yb, zh)
    me_r3 = dev(r3_row, y, r3_z)

    def slot(row, slab, yy, zz):
        return (slab - row + 1) * (2 * Y) + yy * 2 + zz

    size = x_ref.shape[0]
    cuts = [size // chunks * k for k in range(chunks)] + [size]

    def copy(src, slab, yy, zz, to, index, part):
        span = pl.ds(cuts[part], cuts[part + 1] - cuts[part])
        to_slot = slot(to[0], slab, yy, zz)
        return pltpu.make_async_remote_copy(
            src_ref=src.at[span],
            dst_ref=g_ref.at[to_slot, span],
            send_sem=send_sem.at[index, part],
            recv_sem=recv_sem.at[to_slot, part],
            device_id=to,
            device_id_type=MESH,
        )

    def own_copy(to, index, part):
        return copy(x_ref, r, y, zh, to, index, part)

    def relay(slab, yy, zz, to, index, part):
        return copy(g_ref.at[slot(r, slab, yy, zz)], slab, yy, zz, to, index, part)

    def arrived(slab, yy, zz, part):
        span = pl.ds(cuts[part], cuts[part + 1] - cuts[part])
        s = slot(r, slab, yy, zz)
        pltpu.make_async_remote_copy(
            src_ref=g_ref.at[s, span],
            dst_ref=g_ref.at[s, span],
            send_sem=send_sem.at[0, part],
            recv_sem=recv_sem.at[s, part],
            device_id=me_part,
            device_id_type=MESH,
        ).wait_recv()

    own_piece, far_near, far_other, own_other = (r, zh), (far, near_z), (t3, z3), (r, 1 - zh)
    stages = {
        "own_b": (own_piece, yb, False, [(me_yf, 10), (me_part, 11)]),
        "own_f": (own_piece, yf, False, [(me_part, 12)]),
        "own_2": (own_piece, y2, False, [(me_part, 17)]),
        "near_0": (far_near, y, True, [(me_yf, 8), (me_yb, 9)]),
        "near_b": (far_near, yb, True, [(me_yf, 16)]),
        "near_f": (far_near, yf, True, []),
        "near_2": (far_near, y2, True, []),
        "other_0": (far_other, y, False, [(me_yf, 5), (me_yb, 6), (me_r3, 7)]),
        "other_f": (far_other, yf, False, [(me_yb, 13), (me_r3, 15)]),
        "other_b": (far_other, yb, False, [(me_r3, 14)]),
        "other_2": (far_other, y2, False, [(me_r3, 18)]),
        "back_0": (own_other, y, True, [(me_part, 19)]),
        "back_f": (own_other, yf, True, [(me_part, 20)]),
        "back_b": (own_other, yb, True, [(me_part, 21)]),
        "back_2": (own_other, y2, True, [(me_part, 22)]),
    }

    def passed_on(name, part, do):
        (slab, zz), yy, needs_far, targets = stages[name]
        for to, index in targets:
            do(relay(slab, yy, zz, to, index, part))

    def step(name, part):
        (slab, zz), yy, needs_far, _ = stages[name]

        def run():
            arrived(slab, yy, zz, part)
            passed_on(name, part, lambda c: c.start())

        if needs_far:
            pl.when(has_far)(run)
        else:
            run()

    def sent(name, part):
        def run():
            passed_on(name, part, lambda c: c.wait_send())

        if stages[name][2]:
            pl.when(has_far)(run)
        else:
            run()

    groups = ROWS_DEV // 4

    def a_copy(k):
        rows = pl.ds(k * 4, 4)
        return pltpu.make_async_copy(a_hbm.at[rows], a_buf.at[rows], a_sem.at[k])

    def l_copy(k):
        rows = pl.ds(k * 4, 4)
        return pltpu.make_async_copy(l_buf.at[rows], l_hbm.at[rows], l_sem.at[k])

    if with_left:

        @pl.loop(0, groups)
        def _(k):
            a_copy(k).start()

    barrier = pltpu.get_barrier_semaphore()
    for to in (me_other, me_part, me_yf, me_yb):
        pl.semaphore_signal(barrier, inc=1, device_id=to, device_id_type=MESH)

    @pl.when(has_far)
    def _():
        pl.semaphore_signal(barrier, inc=1, device_id=me_near, device_id_type=MESH)

    pl.semaphore_wait(barrier, 4 + has_far.astype(jnp.int32))

    for part in range(chunks):
        @pl.when(has_far)
        def _(part=part):
            own_copy(me_near, 1, part).start()

        own_copy(me_other, 0, part).start()
        own_copy(me_yf, 2, part).start()
        own_copy(me_yb, 3, part).start()
        own_copy(me_part, 4, part).start()

    mine = pltpu.make_async_copy(x_ref, g_ref.at[slot(r, r, y, zh)], own_sem)
    mine.start()

    if with_left:
        low = lax.broadcasted_iota(jnp.int32, (BLK, 128), 1) < BLK
        zero = jnp.zeros((BLK, 128), jnp.bfloat16)

        @pl.loop(0, groups)
        def _(k):
            a_copy(k).wait()
            t0 = x_ref[pl.ds(k * 8, 4)].reshape(BLK, 128)
            t1 = x_ref[pl.ds(k * 8 + 4, 4)].reshape(BLK, 128)
            left_half = jnp.concatenate(
                [jnp.where(low, t0, zero), jnp.where(low, zero, t0), zero, zero], axis=0
            )
            right_half = jnp.concatenate(
                [zero, zero, jnp.where(low, t1, zero), jnp.where(low, zero, t1)], axis=0
            )
            lhs = jnp.concatenate([left_half, right_half], axis=1)
            rows = pl.ds(k * 4, 4)
            for n in range((SLOTS * BLK + 255) // 256):
                width = min(256, SLOTS * BLK - n * 256)
                rhs = a_buf[rows, :, n * 256 : n * 256 + width].reshape(4 * BLK, width)
                prod = lax.dot_general(
                    lhs, rhs, (((0,), (0,)), ((), ())), preferred_element_type=jnp.float32
                ).astype(jnp.bfloat16)
                l_buf[rows, 2 * n] = prod[:, :128].reshape(4, BLK, 128)
                l_buf[rows, 2 * n + 1, :, : width - 128] = prod[:, 128:].reshape(4, BLK, width - 128)
            l_copy(k).start()

    order = sorted((ORDER[name] + part * pace, name, part) for name in stages for part in range(chunks))
    for _, name, part in order:
        step(name, part)

    for yy in range(Y):
        for zz in range(2):
            for part in range(chunks):
                arrived(partner, yy, zz, part)
    mine.wait()

    for part in range(chunks):
        for to, index in ((me_other, 0), (me_yf, 2), (me_yb, 3), (me_part, 4)):
            own_copy(to, index, part).wait_send()

        @pl.when(has_far)
        def _(part=part):
            own_copy(me_near, 1, part).wait_send()

        for name in stages:
            sent(name, part)

    if with_left:

        @pl.loop(0, groups)
        def _(k):
            l_copy(k).wait()


def gather(piece, matrix_blocks, n_rows, with_left=True, chunks=4, pace=2):
    return pl.pallas_call(
        functools.partial(gather_kernel, n_rows, with_left, chunks, pace),
        out_shape=(
            pltpu.HBM((6 * Y,) + piece.shape, piece.dtype),
            pltpu.HBM((ROWS_DEV, PAIRS, BLK, 128), jnp.bfloat16),
        ),
        in_specs=[pl.BlockSpec(memory_space=pltpu.VMEM), pl.BlockSpec(memory_space=pltpu.HBM)],
        out_specs=(pl.BlockSpec(memory_space=pltpu.HBM), pl.BlockSpec(memory_space=pltpu.HBM)),
        scratch_shapes=[
            pltpu.VMEM((ROWS_DEV, BLK, SLOTS * BLK), jnp.bfloat16),
            pltpu.VMEM((ROWS_DEV, PAIRS, BLK, 128), jnp.bfloat16),
            pltpu.SemaphoreType.DMA((23, chunks)),
            pltpu.SemaphoreType.DMA((6 * Y, chunks)),
            pltpu.SemaphoreType.DMA,
            pltpu.SemaphoreType.DMA((ROWS_DEV // 4,)),
            pltpu.SemaphoreType.DMA((ROWS_DEV // 4,)),
        ],
        compiler_params=pltpu.CompilerParams(
            collective_id=0, has_side_effects=True, vmem_limit_bytes=32 << 20
        ),
        name="gather_left",
    )(piece, pltpu.with_memory_space_constraint(matrix_blocks, pltpu.HBM))


def entry_kernel(unroll, n_rows, own_ref, count_ref, slab_ref, col_ref, g_hbm, l_hbm, out_ref, g_ref, agg_ref, l_ref, acc, tab, words, g_sem, agg_sem, l_sem, tab_sem):
    n_dev = 6 * Y
    trash = 2 * AGG_DEV * n_dev
    half = lax.broadcasted_iota(jnp.int32, (BLK, 128), 1) // BLK
    slab = slab_ref[0]
    first = jnp.where(slab > 0, 0, ROWS_DEV * 2 * Y)
    last = jnp.where(slab < n_rows - 1, ROWS_DEV * 6 * Y, ROWS_DEV * 4 * Y)
    groups = ROWS_DEV * PAIRS // 64

    def agg_copy(k):
        return pltpu.make_async_copy(g_hbm.at[k, PIECE - 1], agg_ref.at[k], agg_sem.at[k])

    def g_copy(k):
        return pltpu.make_async_copy(
            g_hbm.at[k, pl.ds(0, PIECE - 1)], g_ref.at[pl.ds(k * (PIECE - 1), PIECE - 1)], g_sem.at[k]
        )

    def l_copy(k):
        span = pl.ds(k * 64, 64)
        return pltpu.make_async_copy(l_hbm.at[span], l_ref.at[span], l_sem.at[k])

    @pl.loop(0, n_dev)
    def _(k):
        agg_copy(k).start()

    @pl.loop(0, n_dev)
    def _(k):
        g_copy(k).start()

    @pl.loop(0, groups)
    def _(k):
        l_copy(k).start()

    lane = lax.broadcasted_iota(jnp.int32, (1, 128), 1)
    spot = lax.broadcasted_iota(jnp.int32, (8, 128), 0) * 128 + lax.broadcasted_iota(jnp.int32, (8, 128), 1)
    cols = jnp.zeros((8, 128), jnp.int32)
    meta = jnp.zeros((8, 128), jnp.int32)
    total = 0
    for i in range(ROWS_DEV):
        begin = total
        total = total + count_ref[i]
        row = jnp.concatenate([col_ref[pl.ds(i, 1), :], jnp.zeros((1, 128 - SLOTS), jnp.int32)], axis=1)
        row = jnp.broadcast_to(pltpu.roll(row, begin & 127, 1), (8, 128))
        here = (spot >= begin) & (spot < total)
        cols = jnp.where(here, row, cols)
        meta = jnp.where(here, (begin << 6) + (own_ref[i] << 5) + i, meta)
    used = spot < total
    slots = spot - (meta >> 6)
    side = cols & 1

    @pl.loop(0, n_dev)
    def _(k):
        agg_copy(k).wait()

    aggs = jnp.zeros((8, 128), jnp.int32)
    for k in range(n_dev // 4):
        row = jnp.zeros((1, 128), jnp.int32)
        for q in range(4):
            tile = agg_ref[4 * k + q].astype(jnp.float32)[:1].astype(jnp.int32)
            row = row + jnp.where(lane // 32 == q, tile & 1, 0)
        row = jnp.broadcast_to(row, (8, 128))
        got = jnp.take_along_axis(row, cols & 127, axis=1, mode="promise_in_bounds")
        aggs = jnp.where(cols >> 7 == k, got, aggs)
    seg = ((meta >> 5) & 1) * (2 * n_dev) + (cols >> 5) * 2 + (aggs ^ side)
    tab[pl.ds(0, 8), :] = jnp.where(used & (cols >= first) & (cols < last), seg, trash)
    tab[pl.ds(8, 8), :] = cols >> 1
    tab[pl.ds(16, 8), :] = jnp.where(used, (meta & 31) * PAIRS + (slots >> 1), ROWS_DEV * PAIRS - 1)
    tab[pl.ds(24, 8), :] = (slots & 1) * BLK
    tab[pl.ds(32, 8), :] = side
    to_words = pltpu.make_async_copy(tab, words, tab_sem)
    to_words.start()

    @pl.loop(0, trash)
    def _(k):
        acc[k] = jnp.zeros((BLK, 128), jnp.float32)

    to_words.wait()

    @pl.loop(0, n_dev)
    def _(k):
        g_copy(k).wait()

    def body(c, ready):
        base = c * unroll
        r0 = base >> 7
        c0 = base & 127
        need = (words[16 + r0, c0 + unroll - 1] >> 6) + 1

        @pl.loop(ready, need)
        def _(k):
            l_copy(k).wait()

        prods = []
        for u in range(unroll):
            right = g_ref[pl.ds(words[8 + r0, c0 + u] * 4, 4)].reshape(BLK, 128)
            left = pltpu.roll(l_ref[words[16 + r0, c0 + u]], words[24 + r0, c0 + u], 1)[:, :BLK]
            prods.append(jnp.dot(left, right, preferred_element_type=jnp.float32))
        for u, prod in enumerate(prods):
            acc[words[r0, c0 + u]] += jnp.where(half == words[32 + r0, c0 + u], prod, 0.0)
        return jnp.maximum(ready, need)

    ready = lax.fori_loop(0, (total + unroll - 1) // unroll, body, 0)

    @pl.loop(ready, groups)
    def _(k):
        l_copy(k).wait()

    for a in range(AGG_DEV):

        @pl.loop(0, n_dev, unroll=6)
        def _(w):
            s = (a * n_dev + w) * 2
            pair = acc[s] + pltpu.roll(acc[s + 1], BLK, 1)
            out_ref[a, :, pl.ds(pl.multiple_of(w * 128, 128), 128)] = pair


def entries(cols, counts, own, slab, gathered, left, n_rows, chunk=128):
    n_dev = 6 * Y
    return pl.pallas_call(
        functools.partial(entry_kernel, chunk, n_rows),
        out_shape=jax.ShapeDtypeStruct((AGG_DEV, BLK, n_dev * AGG_DEV * BLK), jnp.float32),
        in_specs=[pl.BlockSpec(memory_space=pltpu.SMEM)] * 3
        + [pl.BlockSpec(memory_space=pltpu.VMEM)]
        + [pl.BlockSpec(memory_space=pltpu.HBM)] * 2,
        out_specs=pl.BlockSpec(memory_space=pltpu.VMEM),
        scratch_shapes=[
            pltpu.VMEM((n_dev * (PIECE - 1), 16, 128), jnp.bfloat16),
            pltpu.VMEM((n_dev, 16, 128), jnp.bfloat16),
            pltpu.VMEM((ROWS_DEV * PAIRS, BLK, 128), jnp.bfloat16),
            pltpu.VMEM((2 * AGG_DEV * n_dev + 1, BLK, 128), jnp.float32),
            pltpu.VMEM((40, 128), jnp.int32),
            pltpu.SMEM((40, 128), jnp.int32),
            pltpu.SemaphoreType.DMA((n_dev,)),
            pltpu.SemaphoreType.DMA((n_dev,)),
            pltpu.SemaphoreType.DMA((ROWS_DEV * PAIRS // 64,)),
            pltpu.SemaphoreType.DMA,
        ],
        compiler_params=pltpu.CompilerParams(vmem_limit_bytes=44 << 20),
        name="entries",
    )(
        own,
        counts,
        slab,
        cols,
        pltpu.with_memory_space_constraint(gathered, pltpu.HBM),
        pltpu.with_memory_space_constraint(left.reshape(ROWS_DEV * PAIRS, BLK, 128), pltpu.HBM),
    )


def per_device(matrix_blocks, restrict, columns, counts, aggregate):
    n_rows = lax.axis_size("rows")
    slab = lax.axis_index("rows").astype(jnp.int32).reshape(1)
    tiles = restrict.reshape(TILES, 2, BLK, BLK).transpose(0, 3, 1, 2).reshape(TILES * 4, 16, 128)
    agg_tile = jnp.broadcast_to(aggregate.astype(jnp.bfloat16)[None, None, None, :], (1, 16, 4, ROWS_DEV))
    agg_tile = agg_tile.reshape(1, 16, 128)
    piece = jnp.concatenate([tiles, agg_tile], axis=0)
    gathered, left = gather(piece, matrix_blocks, n_rows)
    return entries(columns, counts, aggregate, slab, gathered, left, n_rows)


def solution(mesh):
    return jax.shard_map(
        per_device,
        mesh=mesh,
        in_specs=(
            P(("rows", "cols"), None, None),
            P(("rows", "cols"), None),
            P(("rows", "cols"), None),
            P(("rows", "cols")),
            P(("rows", "cols")),
        ),
        out_specs=P(("rows", "cols"), None, None),
        check_vma=False,
    )
```

```python
import functools

import jax
import jax.numpy as jnp
from jax import lax
from jax.experimental import pallas as pl
from jax.experimental.pallas import tpu as pltpu
from jax.sharding import PartitionSpec as P

BLK = 64
SLOTS = 27
ROWS_DEV = 32
AGG_DEV = 2
Y = 4
NZ = 4
TILES = ROWS_DEV // 2
PIECE = TILES * 4 + 1
PAIRS = (SLOTS + 1) // 2
MESH = pl.DeviceIdType.MESH
ORDER = {
    "own_b": 1, "own_f": 6.5, "other_0": 7.4, "own_2": 12, "other_f": 12.3, "near_0": 14.4, "other_b": 18, "near_b": 21.2,
    "back_b": 21.4, "other_2": 22, "back_0": 25.6, "near_2": 28.5, "back_f": 29.3, "back_2": 34.1, "near_f": 34.4,
}


def gather_kernel(n_rows, with_left, chunks, pace, x_ref, a_hbm, g_ref, l_hbm, a_buf, l_buf, send_sem, recv_sem, own_sem, a_sem, l_sem):
    r = lax.axis_index("rows")
    col = lax.axis_index("cols")
    y = col // 2
    zh = lax.rem(col, 2)
    c = lax.rem(r, 2)
    zlo = lax.rem(r // 2, NZ)
    d = 1 - 2 * c
    partner = r + d
    far = r - d
    has_far = jnp.logical_and(far >= 0, far < n_rows)
    turn = jnp.logical_or(
        jnp.logical_and(zlo == 0, c == 0), jnp.logical_and(zlo == NZ - 1, c == 1)
    ).astype(jnp.int32)
    near_z = lax.rem(zh + turn, 2)
    other_z = 1 - near_z
    t3 = jnp.where(has_far, far, r)
    z3 = jnp.where(has_far, other_z, 1 - zh)
    r3_row = jnp.where(has_far, far, partner)
    r3_z = jnp.where(has_far, near_z, zh)

    def ring(step):
        return lax.rem(y + step + 2 * Y, Y)

    yf, yb, y2 = ring(d), ring(-d), ring(2)

    def dev(row, yy, zz):
        return (row, yy * 2 + zz)

    me_near = dev(far, y, near_z)
    me_other = dev(t3, y, z3)
    me_part = dev(partner, y, zh)
    me_yf = dev(r, yf, zh)
    me_yb = dev(r, yb, zh)
    me_r3 = dev(r3_row, y, r3_z)

    def slot(row, slab, yy, zz):
        return (slab - row + 1) * (2 * Y) + yy * 2 + zz

    size = x_ref.shape[0]
    cuts = [size // chunks * k for k in range(chunks)] + [size]

    def copy(src, slab, yy, zz, to, index, part):
        span = pl.ds(cuts[part], cuts[part + 1] - cuts[part])
        to_slot = slot(to[0], slab, yy, zz)
        return pltpu.make_async_remote_copy(
            src_ref=src.at[span],
            dst_ref=g_ref.at[to_slot, span],
            send_sem=send_sem.at[index, part],
            recv_sem=recv_sem.at[to_slot, part],
            device_id=to,
            device_id_type=MESH,
        )

    def own_copy(to, index, part):
        return copy(x_ref, r, y, zh, to, index, part)

    def relay(slab, yy, zz, to, index, part):
        return copy(g_ref.at[slot(r, slab, yy, zz)], slab, yy, zz, to, index, part)

    def arrived(slab, yy, zz, part):
        span = pl.ds(cuts[part], cuts[part + 1] - cuts[part])
        s = slot(r, slab, yy, zz)
        pltpu.make_async_remote_copy(
            src_ref=g_ref.at[s, span],
            dst_ref=g_ref.at[s, span],
            send_sem=send_sem.at[0, part],
            recv_sem=recv_sem.at[s, part],
            device_id=me_part,
            device_id_type=MESH,
        ).wait_recv()

    own_piece, far_near, far_other, own_other = (r, zh), (far, near_z), (t3, z3), (r, 1 - zh)
    stages = {
        "own_b": (own_piece, yb, False, [(me_yf, 10), (me_part, 11)]),
        "own_f": (own_piece, yf, False, [(me_part, 12)]),
        "own_2": (own_piece, y2, False, [(me_part, 17)]),
        "near_0": (far_near, y, True, [(me_yf, 8), (me_yb, 9)]),
        "near_b": (far_near, yb, True, [(me_yf, 16)]),
        "near_f": (far_near, yf, True, []),
        "near_2": (far_near, y2, True, []),
        "other_0": (far_other, y, False, [(me_yf, 5), (me_yb, 6), (me_r3, 7)]),
        "other_f": (far_other, yf, False, [(me_yb, 13), (me_r3, 15)]),
        "other_b": (far_other, yb, False, [(me_r3, 14)]),
        "other_2": (far_other, y2, False, [(me_r3, 18)]),
        "back_0": (own_other, y, True, [(me_part, 19)]),
        "back_f": (own_other, yf, True, [(me_part, 20)]),
        "back_b": (own_other, yb, True, [(me_part, 21)]),
        "back_2": (own_other, y2, True, [(me_part, 22)]),
    }

    def passed_on(name, part, do):
        (slab, zz), yy, needs_far, targets = stages[name]
        for to, index in targets:
            do(relay(slab, yy, zz, to, index, part))

    def step(name, part):
        (slab, zz), yy, needs_far, _ = stages[name]

        def run():
            arrived(slab, yy, zz, part)
            passed_on(name, part, lambda c: c.start())

        if needs_far:
            pl.when(has_far)(run)
        else:
            run()

    def sent(name, part):
        def run():
            passed_on(name, part, lambda c: c.wait_send())

        if stages[name][2]:
            pl.when(has_far)(run)
        else:
            run()

    groups = ROWS_DEV // 4

    def a_copy(k):
        rows = pl.ds(k * 4, 4)
        return pltpu.make_async_copy(a_hbm.at[rows], a_buf.at[rows], a_sem.at[k])

    def l_copy(k):
        rows = pl.ds(k * 4, 4)
        return pltpu.make_async_copy(l_buf.at[rows], l_hbm.at[rows], l_sem.at[k])

    if with_left:

        @pl.loop(0, groups)
        def _(k):
            a_copy(k).start()

    barrier = pltpu.get_barrier_semaphore()
    for to in (me_other, me_part, me_yf, me_yb):
        pl.semaphore_signal(barrier, inc=1, device_id=to, device_id_type=MESH)

    @pl.when(has_far)
    def _():
        pl.semaphore_signal(barrier, inc=1, device_id=me_near, device_id_type=MESH)

    pl.semaphore_wait(barrier, 4 + has_far.astype(jnp.int32))

    for part in range(chunks):
        own_copy(me_other, 0, part).start()

        @pl.when(has_far)
        def _(part=part):
            own_copy(me_near, 1, part).start()

        own_copy(me_yf, 2, part).start()
        own_copy(me_yb, 3, part).start()
        own_copy(me_part, 4, part).start()

    mine = pltpu.make_async_copy(x_ref, g_ref.at[slot(r, r, y, zh)], own_sem)
    mine.start()

    if with_left:
        low = lax.broadcasted_iota(jnp.int32, (BLK, 128), 1) < BLK
        zero = jnp.zeros((BLK, 128), jnp.bfloat16)

        @pl.loop(0, groups)
        def _(k):
            a_copy(k).wait()
            t0 = x_ref[pl.ds(k * 8, 4)].reshape(BLK, 128)
            t1 = x_ref[pl.ds(k * 8 + 4, 4)].reshape(BLK, 128)
            left_half = jnp.concatenate(
                [jnp.where(low, t0, zero), jnp.where(low, zero, t0), zero, zero], axis=0
            )
            right_half = jnp.concatenate(
                [zero, zero, jnp.where(low, t1, zero), jnp.where(low, zero, t1)], axis=0
            )
            lhs = jnp.concatenate([left_half, right_half], axis=1)
            rows = pl.ds(k * 4, 4)
            for n in range((SLOTS * BLK + 255) // 256):
                width = min(256, SLOTS * BLK - n * 256)
                rhs = a_buf[rows, :, n * 256 : n * 256 + width].reshape(4 * BLK, width)
                prod = lax.dot_general(
                    lhs, rhs, (((0,), (0,)), ((), ())), preferred_element_type=jnp.float32
                ).astype(jnp.bfloat16)
                l_buf[rows, 2 * n] = prod[:, :128].reshape(4, BLK, 128)
                l_buf[rows, 2 * n + 1, :, : width - 128] = prod[:, 128:].reshape(4, BLK, width - 128)
            l_copy(k).start()

    order = sorted((ORDER[name] + part * pace, name, part) for name in stages for part in range(chunks))
    for _, name, part in order:
        step(name, part)

    for yy in range(Y):
        for zz in range(2):
            for part in range(chunks):
                arrived(partner, yy, zz, part)
    mine.wait()

    for part in range(chunks):
        for to, index in ((me_other, 0), (me_yf, 2), (me_yb, 3), (me_part, 4)):
            own_copy(to, index, part).wait_send()

        @pl.when(has_far)
        def _(part=part):
            own_copy(me_near, 1, part).wait_send()

        for name in stages:
            sent(name, part)

    if with_left:

        @pl.loop(0, groups)
        def _(k):
            l_copy(k).wait()


def gather(piece, matrix_blocks, n_rows, with_left=True, chunks=4, pace=2):
    return pl.pallas_call(
        functools.partial(gather_kernel, n_rows, with_left, chunks, pace),
        out_shape=(
            pltpu.HBM((6 * Y,) + piece.shape, piece.dtype),
            pltpu.HBM((ROWS_DEV, PAIRS, BLK, 128), jnp.bfloat16),
        ),
        in_specs=[pl.BlockSpec(memory_space=pltpu.VMEM), pl.BlockSpec(memory_space=pltpu.HBM)],
        out_specs=(pl.BlockSpec(memory_space=pltpu.HBM), pl.BlockSpec(memory_space=pltpu.HBM)),
        scratch_shapes=[
            pltpu.VMEM((ROWS_DEV, BLK, SLOTS * BLK), jnp.bfloat16),
            pltpu.VMEM((ROWS_DEV, PAIRS, BLK, 128), jnp.bfloat16),
            pltpu.SemaphoreType.DMA((23, chunks)),
            pltpu.SemaphoreType.DMA((6 * Y, chunks)),
            pltpu.SemaphoreType.DMA,
            pltpu.SemaphoreType.DMA((ROWS_DEV // 4,)),
            pltpu.SemaphoreType.DMA((ROWS_DEV // 4,)),
        ],
        compiler_params=pltpu.CompilerParams(
            collective_id=0, has_side_effects=True, vmem_limit_bytes=32 << 20
        ),
        name="gather_left",
    )(piece, pltpu.with_memory_space_constraint(matrix_blocks, pltpu.HBM))


def entry_kernel(unroll, n_rows, own_ref, count_ref, slab_ref, col_ref, g_hbm, l_hbm, out_ref, g_ref, agg_ref, l_ref, acc, tab, words, g_sem, agg_sem, l_sem, tab_sem):
    n_dev = 6 * Y
    trash = 2 * AGG_DEV * n_dev
    half = lax.broadcasted_iota(jnp.int32, (BLK, 128), 1) // BLK
    slab = slab_ref[0]
    first = jnp.where(slab > 0, 0, ROWS_DEV * 2 * Y)
    last = jnp.where(slab < n_rows - 1, ROWS_DEV * 6 * Y, ROWS_DEV * 4 * Y)
    groups = ROWS_DEV * PAIRS // 64

    def agg_copy(k):
        return pltpu.make_async_copy(g_hbm.at[k, PIECE - 1], agg_ref.at[k], agg_sem.at[k])

    def g_copy(k):
        return pltpu.make_async_copy(
            g_hbm.at[k, pl.ds(0, PIECE - 1)], g_ref.at[pl.ds(k * (PIECE - 1), PIECE - 1)], g_sem.at[k]
        )

    def l_copy(k):
        span = pl.ds(k * 64, 64)
        return pltpu.make_async_copy(l_hbm.at[span], l_ref.at[span], l_sem.at[k])

    @pl.loop(0, n_dev)
    def _(k):
        agg_copy(k).start()

    @pl.loop(0, n_dev)
    def _(k):
        g_copy(k).start()

    @pl.loop(0, groups)
    def _(k):
        l_copy(k).start()

    lane = lax.broadcasted_iota(jnp.int32, (1, 128), 1)
    spot = lax.broadcasted_iota(jnp.int32, (8, 128), 0) * 128 + lax.broadcasted_iota(jnp.int32, (8, 128), 1)
    cols = jnp.zeros((8, 128), jnp.int32)
    meta = jnp.zeros((8, 128), jnp.int32)
    total = 0
    for i in range(ROWS_DEV):
        begin = total
        total = total + count_ref[i]
        row = jnp.concatenate([col_ref[pl.ds(i, 1), :], jnp.zeros((1, 128 - SLOTS), jnp.int32)], axis=1)
        row = jnp.broadcast_to(pltpu.roll(row, begin & 127, 1), (8, 128))
        here = (spot >= begin) & (spot < total)
        cols = jnp.where(here, row, cols)
        meta = jnp.where(here, (begin << 6) + (own_ref[i] << 5) + i, meta)
    used = spot < total
    slots = spot - (meta >> 6)
    side = cols & 1

    @pl.loop(0, n_dev)
    def _(k):
        agg_copy(k).wait()

    aggs = jnp.zeros((8, 128), jnp.int32)
    for k in range(n_dev // 4):
        row = jnp.zeros((1, 128), jnp.int32)
        for q in range(4):
            tile = agg_ref[4 * k + q].astype(jnp.float32)[:1].astype(jnp.int32)
            row = row + jnp.where(lane // 32 == q, tile & 1, 0)
        row = jnp.broadcast_to(row, (8, 128))
        got = jnp.take_along_axis(row, cols & 127, axis=1, mode="promise_in_bounds")
        aggs = jnp.where(cols >> 7 == k, got, aggs)
    seg = ((meta >> 5) & 1) * (2 * n_dev) + (cols >> 5) * 2 + (aggs ^ side)
    tab[pl.ds(0, 8), :] = jnp.where(used & (cols >= first) & (cols < last), seg, trash)
    tab[pl.ds(8, 8), :] = cols >> 1
    tab[pl.ds(16, 8), :] = jnp.where(used, (meta & 31) * PAIRS + (slots >> 1), ROWS_DEV * PAIRS - 1)
    tab[pl.ds(24, 8), :] = (slots & 1) * BLK
    tab[pl.ds(32, 8), :] = side
    to_words = pltpu.make_async_copy(tab, words, tab_sem)
    to_words.start()

    @pl.loop(0, trash)
    def _(k):
        acc[k] = jnp.zeros((BLK, 128), jnp.float32)

    to_words.wait()

    @pl.loop(0, n_dev)
    def _(k):
        g_copy(k).wait()

    def body(c, ready):
        base = c * unroll
        r0 = base >> 7
        c0 = base & 127
        need = (words[16 + r0, c0 + unroll - 1] >> 6) + 1

        @pl.loop(ready, need)
        def _(k):
            l_copy(k).wait()

        prods = []
        for u in range(unroll):
            right = g_ref[pl.ds(words[8 + r0, c0 + u] * 4, 4)].reshape(BLK, 128)
            left = pltpu.roll(l_ref[words[16 + r0, c0 + u]], words[24 + r0, c0 + u], 1)[:, :BLK]
            prods.append(jnp.dot(left, right, preferred_element_type=jnp.float32))
        for u, prod in enumerate(prods):
            acc[words[r0, c0 + u]] += jnp.where(half == words[32 + r0, c0 + u], prod, 0.0)
        return jnp.maximum(ready, need)

    ready = lax.fori_loop(0, (total + unroll - 1) // unroll, body, 0)

    @pl.loop(ready, groups)
    def _(k):
        l_copy(k).wait()

    for a in range(AGG_DEV):

        @pl.loop(0, n_dev, unroll=6)
        def _(w):
            s = (a * n_dev + w) * 2
            pair = acc[s] + pltpu.roll(acc[s + 1], BLK, 1)
            out_ref[a, :, pl.ds(pl.multiple_of(w * 128, 128), 128)] = pair


def entries(cols, counts, own, slab, gathered, left, n_rows, chunk=128):
    n_dev = 6 * Y
    return pl.pallas_call(
        functools.partial(entry_kernel, chunk, n_rows),
        out_shape=jax.ShapeDtypeStruct((AGG_DEV, BLK, n_dev * AGG_DEV * BLK), jnp.float32),
        in_specs=[pl.BlockSpec(memory_space=pltpu.SMEM)] * 3
        + [pl.BlockSpec(memory_space=pltpu.VMEM)]
        + [pl.BlockSpec(memory_space=pltpu.HBM)] * 2,
        out_specs=pl.BlockSpec(memory_space=pltpu.VMEM),
        scratch_shapes=[
            pltpu.VMEM((n_dev * (PIECE - 1), 16, 128), jnp.bfloat16),
            pltpu.VMEM((n_dev, 16, 128), jnp.bfloat16),
            pltpu.VMEM((ROWS_DEV * PAIRS, BLK, 128), jnp.bfloat16),
            pltpu.VMEM((2 * AGG_DEV * n_dev + 1, BLK, 128), jnp.float32),
            pltpu.VMEM((40, 128), jnp.int32),
            pltpu.SMEM((40, 128), jnp.int32),
            pltpu.SemaphoreType.DMA((n_dev,)),
            pltpu.SemaphoreType.DMA((n_dev,)),
            pltpu.SemaphoreType.DMA((ROWS_DEV * PAIRS // 64,)),
            pltpu.SemaphoreType.DMA,
        ],
        compiler_params=pltpu.CompilerParams(vmem_limit_bytes=44 << 20),
        name="entries",
    )(
        own,
        counts,
        slab,
        cols,
        pltpu.with_memory_space_constraint(gathered, pltpu.HBM),
        pltpu.with_memory_space_constraint(left.reshape(ROWS_DEV * PAIRS, BLK, 128), pltpu.HBM),
    )


def per_device(matrix_blocks, restrict, columns, counts, aggregate):
    n_rows = lax.axis_size("rows")
    slab = lax.axis_index("rows").astype(jnp.int32).reshape(1)
    tiles = jnp.swapaxes(restrict.reshape(TILES, 2 * BLK, BLK), 1, 2).reshape(TILES * 4, 16, 128)
    agg_tile = jnp.broadcast_to(aggregate.astype(jnp.bfloat16)[None, None, None, :], (1, 16, 4, ROWS_DEV))
    agg_tile = agg_tile.reshape(1, 16, 128)
    piece = jnp.concatenate([tiles, agg_tile], axis=0)
    gathered, left = gather(piece, matrix_blocks, n_rows)
    return entries(columns, counts, aggregate, slab, gathered, left, n_rows)


def solution(mesh):
    return jax.shard_map(
        per_device,
        mesh=mesh,
        in_specs=(
            P(("rows", "cols"), None, None),
            P(("rows", "cols"), None),
            P(("rows", "cols"), None),
            P(("rows", "cols")),
            P(("rows", "cols")),
        ),
        out_specs=P(("rows", "cols"), None, None),
        check_vma=False,
    )
```

```python
import functools

import jax
import jax.numpy as jnp
from jax import lax
from jax.experimental import pallas as pl
from jax.experimental.pallas import tpu as pltpu
from jax.sharding import PartitionSpec as P

BLK = 64
SLOTS = 27
ROWS_DEV = 32
AGG_DEV = 2
Y = 4
NZ = 4
TILES = ROWS_DEV // 2
PIECE = TILES * 4 + 1
PAIRS = (SLOTS + 1) // 2
MESH = pl.DeviceIdType.MESH
ORDER = {
    "own_b": 1, "own_f": 6.5, "other_0": 7.4, "own_2": 12, "other_f": 12.3, "near_0": 14.4, "other_b": 18, "near_b": 21.2,
    "back_b": 21.4, "other_2": 22, "back_0": 25.6, "near_2": 28.5, "back_f": 29.3, "back_2": 34.1, "near_f": 34.4,
}


def gather_kernel(n_rows, with_left, chunks, pace, x_ref, a_hbm, g_ref, l_hbm, a_buf, l_buf, send_sem, recv_sem, own_sem, a_sem, l_sem):
    r = lax.axis_index("rows")
    col = lax.axis_index("cols")
    y = col // 2
    zh = lax.rem(col, 2)
    c = lax.rem(r, 2)
    zlo = lax.rem(r // 2, NZ)
    d = 1 - 2 * c
    partner = r + d
    far = r - d
    has_far = jnp.logical_and(far >= 0, far < n_rows)
    turn = jnp.logical_or(
        jnp.logical_and(zlo == 0, c == 0), jnp.logical_and(zlo == NZ - 1, c == 1)
    ).astype(jnp.int32)
    near_z = lax.rem(zh + turn, 2)
    other_z = 1 - near_z
    t3 = jnp.where(has_far, far, r)
    z3 = jnp.where(has_far, other_z, 1 - zh)
    r3_row = jnp.where(has_far, far, partner)
    r3_z = jnp.where(has_far, near_z, zh)

    def ring(step):
        return lax.rem(y + step + 2 * Y, Y)

    yf, yb, y2 = ring(d), ring(-d), ring(2)

    def dev(row, yy, zz):
        return (row, yy * 2 + zz)

    me_near = dev(far, y, near_z)
    me_other = dev(t3, y, z3)
    me_part = dev(partner, y, zh)
    me_yf = dev(r, yf, zh)
    me_yb = dev(r, yb, zh)
    me_r3 = dev(r3_row, y, r3_z)

    def slot(row, slab, yy, zz):
        return (slab - row + 1) * (2 * Y) + yy * 2 + zz

    size = x_ref.shape[0]
    cuts = [size // chunks * k for k in range(chunks)] + [size]

    def copy(src, slab, yy, zz, to, index, part):
        span = pl.ds(cuts[part], cuts[part + 1] - cuts[part])
        to_slot = slot(to[0], slab, yy, zz)
        return pltpu.make_async_remote_copy(
            src_ref=src.at[span],
            dst_ref=g_ref.at[to_slot, span],
            send_sem=send_sem.at[index, part],
            recv_sem=recv_sem.at[to_slot, part],
            device_id=to,
            device_id_type=MESH,
        )

    def own_copy(to, index, part):
        return copy(x_ref, r, y, zh, to, index, part)

    def relay(slab, yy, zz, to, index, part):
        return copy(g_ref.at[slot(r, slab, yy, zz)], slab, yy, zz, to, index, part)

    def arrived(slab, yy, zz, part):
        span = pl.ds(cuts[part], cuts[part + 1] - cuts[part])
        s = slot(r, slab, yy, zz)
        pltpu.make_async_remote_copy(
            src_ref=g_ref.at[s, span],
            dst_ref=g_ref.at[s, span],
            send_sem=send_sem.at[0, part],
            recv_sem=recv_sem.at[s, part],
            device_id=me_part,
            device_id_type=MESH,
        ).wait_recv()

    own_piece, far_near, far_other, own_other = (r, zh), (far, near_z), (t3, z3), (r, 1 - zh)
    stages = {
        "own_b": (own_piece, yb, False, [(me_yf, 10), (me_part, 11)]),
        "own_f": (own_piece, yf, False, [(me_part, 12)]),
        "own_2": (own_piece, y2, False, [(me_part, 17)]),
        "near_0": (far_near, y, True, [(me_yf, 8), (me_yb, 9)]),
        "near_b": (far_near, yb, True, [(me_yf, 16)]),
        "near_f": (far_near, yf, True, []),
        "near_2": (far_near, y2, True, []),
        "other_0": (far_other, y, False, [(me_yf, 5), (me_yb, 6), (me_r3, 7)]),
        "other_f": (far_other, yf, False, [(me_yb, 13), (me_r3, 15)]),
        "other_b": (far_other, yb, False, [(me_r3, 14)]),
        "other_2": (far_other, y2, False, [(me_r3, 18)]),
        "back_0": (own_other, y, True, [(me_part, 19)]),
        "back_f": (own_other, yf, True, [(me_part, 20)]),
        "back_b": (own_other, yb, True, [(me_part, 21)]),
        "back_2": (own_other, y2, True, [(me_part, 22)]),
    }

    def passed_on(name, part, do):
        (slab, zz), yy, needs_far, targets = stages[name]
        for to, index in targets:
            do(relay(slab, yy, zz, to, index, part))

    def step(name, part):
        (slab, zz), yy, needs_far, _ = stages[name]

        def run():
            arrived(slab, yy, zz, part)
            passed_on(name, part, lambda c: c.start())

        if needs_far:
            pl.when(has_far)(run)
        else:
            run()

    def sent(name, part):
        def run():
            passed_on(name, part, lambda c: c.wait_send())

        if stages[name][2]:
            pl.when(has_far)(run)
        else:
            run()

    groups = ROWS_DEV // 4

    def a_copy(k):
        rows = pl.ds(k * 4, 4)
        return pltpu.make_async_copy(a_hbm.at[rows], a_buf.at[rows], a_sem.at[k])

    def l_copy(k):
        rows = pl.ds(k * 4, 4)
        return pltpu.make_async_copy(l_buf.at[rows], l_hbm.at[rows], l_sem.at[k])

    if with_left:

        @pl.loop(0, groups)
        def _(k):
            a_copy(k).start()

    barrier = pltpu.get_barrier_semaphore()
    for to in (me_other, me_part, me_yf, me_yb):
        pl.semaphore_signal(barrier, inc=1, device_id=to, device_id_type=MESH)

    @pl.when(has_far)
    def _():
        pl.semaphore_signal(barrier, inc=1, device_id=me_near, device_id_type=MESH)

    pl.semaphore_wait(barrier, 4 + has_far.astype(jnp.int32))

    for part in range(chunks):
        own_copy(me_other, 0, part).start()

        @pl.when(has_far)
        def _(part=part):
            own_copy(me_near, 1, part).start()

        own_copy(me_yf, 2, part).start()
        own_copy(me_yb, 3, part).start()
        own_copy(me_part, 4, part).start()

    mine = pltpu.make_async_copy(x_ref, g_ref.at[slot(r, r, y, zh)], own_sem)
    mine.start()

    if with_left:
        low = lax.broadcasted_iota(jnp.int32, (BLK, 128), 1) < BLK
        zero = jnp.zeros((BLK, 128), jnp.bfloat16)

        @pl.loop(0, groups)
        def _(k):
            a_copy(k).wait()
            t0 = x_ref[pl.ds(k * 8, 4)].reshape(BLK, 128)
            t1 = x_ref[pl.ds(k * 8 + 4, 4)].reshape(BLK, 128)
            left_half = jnp.concatenate(
                [jnp.where(low, t0, zero), jnp.where(low, zero, t0), zero, zero], axis=0
            )
            right_half = jnp.concatenate(
                [zero, zero, jnp.where(low, t1, zero), jnp.where(low, zero, t1)], axis=0
            )
            lhs = jnp.concatenate([left_half, right_half], axis=1)
            rows = pl.ds(k * 4, 4)
            for n in range((SLOTS * BLK + 255) // 256):
                width = min(256, SLOTS * BLK - n * 256)
                rhs = a_buf[rows, :, n * 256 : n * 256 + width].reshape(4 * BLK, width)
                prod = lax.dot_general(
                    lhs, rhs, (((0,), (0,)), ((), ())), preferred_element_type=jnp.float32
                ).astype(jnp.bfloat16)
                l_buf[rows, 2 * n] = prod[:, :128].reshape(4, BLK, 128)
                l_buf[rows, 2 * n + 1, :, : width - 128] = prod[:, 128:].reshape(4, BLK, width - 128)
            l_copy(k).start()

    order = sorted((ORDER[name] + part * pace, name, part) for name in stages for part in range(chunks))
    for _, name, part in order:
        step(name, part)

    for yy in range(Y):
        for zz in range(2):
            for part in range(chunks):
                arrived(partner, yy, zz, part)
    mine.wait()

    for part in range(chunks):
        for to, index in ((me_other, 0), (me_yf, 2), (me_yb, 3), (me_part, 4)):
            own_copy(to, index, part).wait_send()

        @pl.when(has_far)
        def _(part=part):
            own_copy(me_near, 1, part).wait_send()

        for name in stages:
            sent(name, part)

    if with_left:

        @pl.loop(0, groups)
        def _(k):
            l_copy(k).wait()


def gather(piece, matrix_blocks, n_rows, with_left=True, chunks=4, pace=2):
    return pl.pallas_call(
        functools.partial(gather_kernel, n_rows, with_left, chunks, pace),
        out_shape=(
            pltpu.HBM((6 * Y,) + piece.shape, piece.dtype),
            pltpu.HBM((ROWS_DEV, PAIRS, BLK, 128), jnp.bfloat16),
        ),
        in_specs=[pl.BlockSpec(memory_space=pltpu.VMEM), pl.BlockSpec(memory_space=pltpu.HBM)],
        out_specs=(pl.BlockSpec(memory_space=pltpu.HBM), pl.BlockSpec(memory_space=pltpu.HBM)),
        scratch_shapes=[
            pltpu.VMEM((ROWS_DEV, BLK, SLOTS * BLK), jnp.bfloat16),
            pltpu.VMEM((ROWS_DEV, PAIRS, BLK, 128), jnp.bfloat16),
            pltpu.SemaphoreType.DMA((23, chunks)),
            pltpu.SemaphoreType.DMA((6 * Y, chunks)),
            pltpu.SemaphoreType.DMA,
            pltpu.SemaphoreType.DMA((ROWS_DEV // 4,)),
            pltpu.SemaphoreType.DMA((ROWS_DEV // 4,)),
        ],
        compiler_params=pltpu.CompilerParams(
            collective_id=0, has_side_effects=True, vmem_limit_bytes=32 << 20
        ),
        name="gather_left",
    )(piece, pltpu.with_memory_space_constraint(matrix_blocks, pltpu.HBM))


def entry_kernel(unroll, n_rows, own_ref, count_ref, slab_ref, col_ref, g_hbm, l_hbm, out_hbm, out_ref, out_sem, g_ref, agg_ref, l_ref, acc, tab, words, g_sem, agg_sem, l_sem, tab_sem):
    n_dev = 6 * Y
    trash = 2 * AGG_DEV * n_dev
    half = lax.broadcasted_iota(jnp.int32, (BLK, 128), 1) // BLK
    slab = slab_ref[0]
    first = jnp.where(slab > 0, 0, ROWS_DEV * 2 * Y)
    last = jnp.where(slab < n_rows - 1, ROWS_DEV * 6 * Y, ROWS_DEV * 4 * Y)
    groups = ROWS_DEV * PAIRS // 64

    def agg_copy(k):
        return pltpu.make_async_copy(g_hbm.at[k, PIECE - 1], agg_ref.at[k], agg_sem.at[k])

    def g_copy(k):
        return pltpu.make_async_copy(
            g_hbm.at[k, pl.ds(0, PIECE - 1)], g_ref.at[pl.ds(k * (PIECE - 1), PIECE - 1)], g_sem.at[k]
        )

    def l_copy(k):
        span = pl.ds(k * 64, 64)
        return pltpu.make_async_copy(l_hbm.at[span], l_ref.at[span], l_sem.at[k])

    @pl.loop(0, n_dev)
    def _(k):
        agg_copy(k).start()

    @pl.loop(0, n_dev)
    def _(k):
        g_copy(k).start()

    @pl.loop(0, groups)
    def _(k):
        l_copy(k).start()

    lane = lax.broadcasted_iota(jnp.int32, (1, 128), 1)
    spot = lax.broadcasted_iota(jnp.int32, (8, 128), 0) * 128 + lax.broadcasted_iota(jnp.int32, (8, 128), 1)
    cols = jnp.zeros((8, 128), jnp.int32)
    meta = jnp.zeros((8, 128), jnp.int32)
    total = 0
    for i in range(ROWS_DEV):
        begin = total
        total = total + count_ref[i]
        row = jnp.concatenate([col_ref[pl.ds(i, 1), :], jnp.zeros((1, 128 - SLOTS), jnp.int32)], axis=1)
        row = jnp.broadcast_to(pltpu.roll(row, begin & 127, 1), (8, 128))
        here = (spot >= begin) & (spot < total)
        cols = jnp.where(here, row, cols)
        meta = jnp.where(here, (begin << 6) + (own_ref[i] << 5) + i, meta)
    used = spot < total
    slots = spot - (meta >> 6)
    side = cols & 1

    @pl.loop(0, n_dev)
    def _(k):
        agg_copy(k).wait()

    aggs = jnp.zeros((8, 128), jnp.int32)
    for k in range(n_dev // 4):
        row = jnp.zeros((1, 128), jnp.int32)
        for q in range(4):
            tile = agg_ref[4 * k + q].astype(jnp.float32)[:1].astype(jnp.int32)
            row = row + jnp.where(lane // 32 == q, tile & 1, 0)
        row = jnp.broadcast_to(row, (8, 128))
        got = jnp.take_along_axis(row, cols & 127, axis=1, mode="promise_in_bounds")
        aggs = jnp.where(cols >> 7 == k, got, aggs)
    seg = ((meta >> 5) & 1) * (2 * n_dev) + (cols >> 5) * 2 + (aggs ^ side)
    tab[pl.ds(0, 8), :] = jnp.where(used & (cols >= first) & (cols < last), seg, trash)
    tab[pl.ds(8, 8), :] = cols >> 1
    tab[pl.ds(16, 8), :] = jnp.where(used, (meta & 31) * PAIRS + (slots >> 1), ROWS_DEV * PAIRS - 1)
    tab[pl.ds(24, 8), :] = (slots & 1) * BLK
    tab[pl.ds(32, 8), :] = side
    to_words = pltpu.make_async_copy(tab, words, tab_sem)
    to_words.start()

    @pl.loop(0, trash)
    def _(k):
        acc[k] = jnp.zeros((BLK, 128), jnp.float32)

    to_words.wait()

    @pl.loop(0, n_dev)
    def _(k):
        g_copy(k).wait()

    def body(c, ready):
        base = c * unroll
        r0 = base >> 7
        c0 = base & 127
        need = (words[16 + r0, c0 + unroll - 1] >> 6) + 1

        @pl.loop(ready, need)
        def _(k):
            l_copy(k).wait()

        prods = []
        for u in range(unroll):
            right = g_ref[pl.ds(words[8 + r0, c0 + u] * 4, 4)].reshape(BLK, 128)
            left = l_ref[words[16 + r0, c0 + u]]
            left = jnp.where(half * BLK == words[24 + r0, c0 + u], left, jnp.bfloat16(0))
            right = jnp.concatenate([right, right], axis=0)
            prods.append(jnp.dot(left, right, preferred_element_type=jnp.float32))
        for u, prod in enumerate(prods):
            acc[words[r0, c0 + u]] += jnp.where(half == words[32 + r0, c0 + u], prod, 0.0)
        return jnp.maximum(ready, need)

    ready = lax.fori_loop(0, (total + unroll - 1) // unroll, body, 0)

    @pl.loop(ready, groups)
    def _(k):
        l_copy(k).wait()

    for a in range(AGG_DEV):

        @pl.loop(0, n_dev, unroll=6)
        def _(w):
            s = (a * n_dev + w) * 2
            pair = acc[s] + pltpu.roll(acc[s + 1], BLK, 1)
            out_ref[a, :, pl.ds(pl.multiple_of(w * 128, 128), 128)] = pair

        pltpu.make_async_copy(out_ref.at[a], out_hbm.at[a], out_sem.at[a]).start()

    for a in range(AGG_DEV):
        pltpu.make_async_copy(out_ref.at[a], out_hbm.at[a], out_sem.at[a]).wait()


def entries(cols, counts, own, slab, gathered, left, n_rows, chunk=128):
    n_dev = 6 * Y
    return pl.pallas_call(
        functools.partial(entry_kernel, chunk, n_rows),
        out_shape=pltpu.HBM((AGG_DEV, BLK, n_dev * AGG_DEV * BLK), jnp.float32),
        in_specs=[pl.BlockSpec(memory_space=pltpu.SMEM)] * 3
        + [pl.BlockSpec(memory_space=pltpu.VMEM)]
        + [pl.BlockSpec(memory_space=pltpu.HBM)] * 2,
        out_specs=pl.BlockSpec(memory_space=pltpu.HBM),
        scratch_shapes=[
            pltpu.VMEM((AGG_DEV, BLK, n_dev * AGG_DEV * BLK), jnp.float32),
            pltpu.SemaphoreType.DMA((AGG_DEV,)),
            pltpu.VMEM((n_dev * (PIECE - 1), 16, 128), jnp.bfloat16),
            pltpu.VMEM((n_dev, 16, 128), jnp.bfloat16),
            pltpu.VMEM((ROWS_DEV * PAIRS, BLK, 128), jnp.bfloat16),
            pltpu.VMEM((2 * AGG_DEV * n_dev + 1, BLK, 128), jnp.float32),
            pltpu.VMEM((40, 128), jnp.int32),
            pltpu.SMEM((40, 128), jnp.int32),
            pltpu.SemaphoreType.DMA((n_dev,)),
            pltpu.SemaphoreType.DMA((n_dev,)),
            pltpu.SemaphoreType.DMA((ROWS_DEV * PAIRS // 64,)),
            pltpu.SemaphoreType.DMA,
        ],
        compiler_params=pltpu.CompilerParams(vmem_limit_bytes=44 << 20),
        name="entries",
    )(
        own,
        counts,
        slab,
        cols,
        pltpu.with_memory_space_constraint(gathered, pltpu.HBM),
        pltpu.with_memory_space_constraint(left.reshape(ROWS_DEV * PAIRS, BLK, 128), pltpu.HBM),
    )


def per_device(matrix_blocks, restrict, columns, counts, aggregate):
    n_rows = lax.axis_size("rows")
    slab = lax.axis_index("rows").astype(jnp.int32).reshape(1)
    tiles = jnp.swapaxes(restrict.reshape(TILES, 2 * BLK, BLK), 1, 2).reshape(TILES * 4, 16, 128)
    agg_tile = jnp.broadcast_to(aggregate.astype(jnp.bfloat16)[None, None, None, :], (1, 16, 4, ROWS_DEV))
    agg_tile = agg_tile.reshape(1, 16, 128)
    piece = jnp.concatenate([tiles, agg_tile], axis=0)
    gathered, left = gather(piece, matrix_blocks, n_rows)
    return entries(columns, counts, aggregate, slab, gathered, left, n_rows)


def solution(mesh):
    return jax.shard_map(
        per_device,
        mesh=mesh,
        in_specs=(
            P(("rows", "cols"), None, None),
            P(("rows", "cols"), None),
            P(("rows", "cols"), None),
            P(("rows", "cols")),
            P(("rows", "cols")),
        ),
        out_specs=P(("rows", "cols"), None, None),
        check_vma=False,
    )
```
